32 devices in a mesh: row: 4 (over y, core), blk: 8 (over z, x).
Axes of the slice: x: 2, y: 2, z: 4, core: 2. Of those that a mesh axis runs over, the one named last changes fastest.
Arguments:
- matrix: float32 [16384, 2048], P('row', 'blk'), may hold values from -6 to 6
Outputs:
- rotated: float32 [16384, 2048], P('row', 'blk')
- off_measure: float32 [2], replicated
The draws below stay inside these ranges and needn't reach their ends.
All inputs are finite; a program needn't handle non-finite values.
Results may differ from the reference program's by a relative error of at most 0.00012.
Values sent between devices are 32-bit elements; how exact they have to be, the bound alone decides.
A program may use at most 64 MiB of HBM per device.

```python
import jax
import jax.numpy as jnp
from jax import lax

B = 128
STEPS = 2
NS_ITERS = 4
ROWS = 16384
NCOLS = 2048
N_BLK = 8


def levels(own_key, extent, cuts, least, largest):
    def one(dim, parts):
        draws = jax.random.uniform(jax.random.fold_in(jax.random.fold_in(own_key, 6), dim), (parts,), jnp.float32, least / len(cuts), largest / len(cuts))
        return jnp.repeat(jnp.exp(draws), extent[dim] // parts).reshape((-1,) + (1,) * (len(extent) - dim - 1))

    factor_of = one(*cuts[0])
    for cut in cuts[1:]:
        factor_of = factor_of * one(*cut)
    return factor_of


def bell_draw(stream_key, shape, spread, reach, split=(), kind=jnp.bfloat16):
    entries = jax.random.normal(stream_key, shape, jnp.float32) * spread
    if len(split) > 0:
        entries = levels(stream_key, shape, split, -0.22, 0.18) * entries
    return jnp.clip(entries, min=-reach, max=reach).astype(kind)


def setup_inputs(seed: int = 0) -> dict:
    streams_of = jax.random.split(jax.random.key(seed), 2)
    return {
        "matrix": bell_draw(streams_of[0], (ROWS, NCOLS), 1.0, 6.0, ((0, 4), (1, 8)), jnp.float32),
    }


HIGH = lax.Precision.HIGHEST

def inverse_root(square, bound_scale):
    identity = jnp.eye(square.shape[0], dtype=jnp.float32)
    current = square / bound_scale
    result = identity
    for count_index in range(NS_ITERS):
        factor = 1.5 * identity - 0.5 * jnp.dot(result, current, precision=HIGH)
        current = jnp.dot(current, factor, precision=HIGH)
        result = jnp.dot(factor, result, precision=HIGH)
    return result / jnp.sqrt(bound_scale)

def reference(matrix):
    blocks = matrix.reshape(ROWS, N_BLK, 2, B)
    left_block = blocks[:, :, 0]
    right_block = blocks[:, :, 1]
    identity = jnp.eye(B, dtype=jnp.float32)
    norm_list = []
    for step_index in range(STEPS):
        cross_gram = jnp.einsum('rpi,rpj->pij', left_block, right_block, precision=HIGH)
        first_norms = lax.optimization_barrier(jnp.sum(left_block * left_block, axis=0))
        second_norms = lax.optimization_barrier(jnp.sum(right_block * right_block, axis=0))
        cosines = cross_gram * lax.rsqrt(first_norms)[:, :, None] * lax.rsqrt(second_norms)[:, None, :]
        norm_list.append(jnp.mean(lax.optimization_barrier(jnp.sum(cosines * cosines, axis=(1, 2)))))
        coupling = 0.5 * cosines
        bound_scale = 1.0 + lax.optimization_barrier(jnp.sum(coupling * coupling, axis=(1, 2)))
        first_square = identity + jnp.einsum('pij,pkj->pik', coupling, coupling, precision=HIGH)
        second_square = identity + jnp.einsum('pji,pjk->pik', coupling, coupling, precision=HIGH)
        first_root = jax.vmap(inverse_root)(first_square, bound_scale)
        second_root = jax.vmap(inverse_root)(second_square, bound_scale)
        mixed_left = left_block - jnp.einsum('rpj,pij->rpi', right_block, coupling, precision=HIGH)
        mixed_right = right_block + jnp.einsum('rpi,pij->rpj', left_block, coupling, precision=HIGH)
        new_left = jnp.einsum('rpi,pij->rpj', mixed_left, first_root, precision=HIGH)
        new_right = jnp.einsum('rpi,pij->rpj', mixed_right, second_root, precision=HIGH)
        if step_index % 2 == 0:
            left_block = jnp.roll(new_left, 1, axis=1)
            right_block = new_right
        else:
            left_block = new_left
            right_block = jnp.roll(new_right, 1, axis=1)
    rotated = jnp.stack([left_block, right_block], axis=2).reshape(ROWS, 2 * B * N_BLK)
    return (rotated, jnp.stack(norm_list))
```

```python
import functools

import jax
import jax.numpy as jnp
from jax import lax
from jax.experimental import pallas as pl
from jax.experimental.pallas import tpu as pltpu
from jax.sharding import PartitionSpec as P

STEPS = 2
NS_ITERS = 4
MESH = pl.DeviceIdType.MESH
F32 = jnp.float32
BF16 = jnp.bfloat16


def split(value):
    high = value.astype(BF16)
    return high, (value - high.astype(F32)).astype(BF16)


def dot(a, b):
    return jnp.dot(a, b, preferred_element_type=F32)


def product(a, b):
    ah, al = split(a)
    bh, bl = split(b)
    width = b.shape[1]
    both = dot(
        jnp.concatenate([ah, al], axis=1),
        jnp.concatenate(
            [
                jnp.concatenate([bh, bl], axis=1),
                jnp.concatenate([bh, jnp.zeros_like(bl)], axis=1),
            ],
            axis=0,
        ),
    )
    return both[:, :width] + both[:, width:]


def mixing(cosines):
    width = cosines.shape[0]
    rows = lax.broadcasted_iota(jnp.int32, (width, width), 0)
    columns = lax.broadcasted_iota(jnp.int32, (width, width), 1)
    identity = jnp.where(rows == columns, 1.0, 0.0).astype(F32)
    coupling = 0.5 * cosines
    flipped = coupling.T
    scale = 1.0 + jnp.sum(coupling * coupling, keepdims=True)
    shrink = 1.0 / scale
    current = [
        (identity + product(coupling, flipped)) * shrink,
        (identity + product(flipped, coupling)) * shrink,
    ]
    result = [None, None]
    for count in range(NS_ITERS):
        for side in range(2):
            y, z = current[side], result[side]
            inner = y if z is None else product(z, y)
            factor = 1.5 * identity - 0.5 * inner
            if count < NS_ITERS - 1:
                current[side] = product(y, factor)
            result[side] = factor if z is None else product(factor, z)
    root = 1.0 / jnp.sqrt(scale)
    first, second = result[0] * root, result[1] * root
    return (
        jnp.concatenate([first, product(coupling, second)], axis=1),
        jnp.concatenate([-product(flipped, first), second], axis=1),
    )


def kernel(
    row_count, blk_count, plan, x_hbm, out_ref, off_ref,
    xv, move0, stay0, come0, rest, move1, raw, via, skip, hold,
    acc, norms, gath, weights, coses, cosin, mgath,
    load_sem, via_recv, hold_recv, first_recv, row_send, row_recv, send, recv, hello, up, down,
):
    rows, both = x_hbm.shape
    width = both // 2
    chunks, loads, early, given_even, given_odd, pieces, ahead_last = plan
    ahead, before_first, after_first = pieces
    chunk, gram_chunk = rows // chunks, rows // loads
    widen = up.shape[0]
    share = width // row_count
    row, blk = lax.axis_index("row"), lax.axis_index("blk")
    after = lax.rem(blk + 1, blk_count)
    second = lax.rem(blk + 2, blk_count)
    below = lax.rem(blk + blk_count - 1, blk_count)
    odd = lax.rem(blk, 2) == 1
    even = jnp.logical_not(odd)
    last = blk == blk_count - 1
    inner = jnp.logical_and(odd, jnp.logical_not(last))
    passing = jnp.where(odd, given_even, given_odd)
    given = jnp.where(odd, given_odd, given_even)

    barrier = pltpu.get_barrier_semaphore()
    for k in range(1, row_count):
        pl.semaphore_signal(
            barrier, inc=1, device_id={"row": lax.rem(row + k, row_count)}, device_id_type=MESH
        )
    pl.semaphore_signal(barrier, inc=1, device_id={"blk": below}, device_id_type=MESH)

    def at(i, size):
        return pl.ds(pl.multiple_of(i * size, size), size)

    def span(first, last):
        return pl.ds(int(first * chunk), int((last - first) * chunk))

    def load(i):
        return pltpu.make_async_copy(
            x_hbm.at[at(i, gram_chunk)], xv.at[at(i, gram_chunk)], load_sem.at[i]
        )

    def start_load(i, carry):
        load(i).start()
        return carry

    lax.fori_loop(0, rows // gram_chunk, start_load, 0)

    def to_blk(source, target, send, recv, peer):
        return pltpu.make_async_remote_copy(
            src_ref=source, dst_ref=target, send_sem=send, recv_sem=recv,
            device_id={"blk": peer}, device_id_type=MESH,
        )

    RAW, SKIP, REST, SECOND, MEASURE, COS, FIRST, ON = 0, 1, 2, 3, 4, 5, 5 + STEPS, 6 + STEPS
    right = pl.ds(width, width)

    def raw_next(part):
        return to_blk(xv.at[part], raw.at[part], send.at[RAW], recv.at[RAW], after)

    def raw_below(part, i):
        return to_blk(xv.at[part], via.at[part], send.at[RAW], via_recv.at[i], below)

    def raw_on(part):
        return to_blk(via.at[part], raw.at[part], send.at[ON], recv.at[RAW], second)

    def skip_move(part):
        return to_blk(move0.at[part], skip.at[part], send.at[SKIP], recv.at[SKIP], second)

    def first_move(part, i):
        return to_blk(
            move0.at[part], come0.at[part], send.at[FIRST], first_recv.at[i - early], after
        )

    def second_move(part):
        return to_blk(
            move1.at[part], out_ref.at[part, right], send.at[SECOND], recv.at[SECOND], after
        )

    def give_move(part):
        return to_blk(stay0.at[part], rest.at[part], send.at[REST], recv.at[REST], after)

    def hold_move(part, i):
        return to_blk(stay0.at[part], hold.at[part], send.at[REST], hold_recv.at[i - early], below)

    def pass_move(part):
        return to_blk(hold.at[part], rest.at[part], send.at[ON + 1], recv.at[REST], second)

    def cos_move(step):
        part = at(row, share)
        return to_blk(
            coses.at[step, part], cosin.at[step, part], send.at[COS + step], recv.at[COS + step],
            after,
        )

    def cos_copy(step, part, peer):
        return pltpu.make_async_remote_copy(
            src_ref=cosin.at[step, part], dst_ref=cosin.at[step, part],
            send_sem=row_send.at[0], recv_sem=row_recv.at[STEPS + step],
            device_id={"row": peer}, device_id_type=MESH,
        )

    def message(part, peer):
        return to_blk(mgath.at[part], mgath.at[part], send.at[MEASURE], recv.at[MEASURE], peer)

    def tell_in(semaphore, peer):
        pl.semaphore_signal(semaphore, inc=1, device_id={"blk": peer}, device_id_type=MESH)

    def round_start(k):
        tell_in(up.at[k], lax.rem(blk + 2**k, blk_count))
        tell_in(down.at[k], lax.rem(blk + blk_count - 2**k, blk_count))

    def round_end(k):
        pl.semaphore_wait(up.at[k], 1)
        pl.semaphore_wait(down.at[k], 1)

    pl.semaphore_wait(barrier, row_count)
    tell_in(hello.at[0], after)
    for i in range(-(-early * loads // chunks)):
        load(i).wait()

    @pl.when(even)
    def _():
        for i in range(early):
            raw_next(span(i, i + 1)).start()

    @pl.when(odd)
    def _():
        pl.semaphore_wait(hello.at[0], 1)
        for i in range(early):
            raw_below(span(i, i + 1), i).start()

    def add_gram(left, right):
        lh, ll = split(left)
        rh, rl = split(right)
        acc[...] += lax.dot_general(
            jnp.concatenate([lh, ll], axis=1),
            jnp.concatenate([rh, rl], axis=1),
            (((0,), (0,)), ((), ())),
            preferred_element_type=F32,
        )
        norms[0:8] += jnp.sum((left * left).reshape(-1, 8, width), axis=0)
        norms[8:16] += jnp.sum((right * right).reshape(-1, 8, width), axis=0)

    def clear():
        acc[...] = jnp.zeros_like(acc)
        norms[...] = jnp.zeros_like(norms)

    def mix(slot, cosines):
        top, bottom = mixing(cosines)
        high, low = split(top)
        weights[slot, 0, :width] = high
        weights[slot, 1, :width] = low
        high, low = split(bottom)
        weights[slot, 0, width:] = high
        weights[slot, 1, width:] = low

    lane = lax.broadcasted_iota(jnp.int32, (1, width), 1)

    def row_peer(k):
        return lax.rem(row + k, row_count)

    def exchange(step):
        def copy(owners, peer):
            return pltpu.make_async_remote_copy(
                src_ref=gath.at[step, owners], dst_ref=gath.at[step, owners],
                send_sem=row_send.at[0], recv_sem=row_recv.at[step],
                device_id={"row": peer}, device_id_type=MESH,
            )

        gath[step, row, 0:width] = (
            acc[:width, :width] + acc[:width, width:] + acc[width:, :width]
        ) + acc[width:, width:]
        first = jnp.sum(norms[0:8], axis=0, keepdims=True)
        second = jnp.sum(norms[8:16], axis=0, keepdims=True)
        gath[step, row, width:width + 8] = jnp.broadcast_to(first, (8, width))
        gath[step, row, width + 8:width + 16] = jnp.broadcast_to(second, (8, width))
        for k in range(1, row_count):
            copy(pl.ds(row, 1), row_peer(k)).start()
        all_copies = copy(pl.ds(0, row_count - 1), row_peer(1))
        all_copies.wait_recv()
        total = gath[step, 0]
        for r in range(1, row_count):
            total = total + gath[step, r]
        all_copies.wait_send()
        cross = total[:width]
        first = lax.rsqrt(jnp.broadcast_to(total[width:width + 1], (width, width))).T
        second = lax.rsqrt(jnp.broadcast_to(total[width + 8:width + 9], (width, width)))
        cosines = cross * first * second
        coses[step] = cosines
        cos_move(step).start()
        mix(0, cosines)
        summed = jnp.sum(cosines * cosines, keepdims=True)
        own = jnp.where(lane == step, jnp.broadcast_to(summed, (1, width)), 0.0)
        if step == 0:
            mgath[blk] = own
        else:
            mgath[blk] += own

    def mix_below(step):
        cos_move(step).wait_recv()
        for k in range(1, row_count):
            cos_copy(step, at(row, share), row_peer(k)).start()
        all_copies = cos_copy(step, pl.ds(0, (row_count - 1) * share), row_peer(1))
        all_copies.wait_recv()
        mix(1, cosin[step])
        all_copies.wait_send()

    def transform(slot, left, right):
        lh, ll = split(left)
        rh, rl = split(right)
        high = jnp.concatenate([lh, rh], axis=1)
        low = jnp.concatenate([ll, rl], axis=1)
        own, fine = weights[slot, 0], weights[slot, 1]
        return dot(high, own) + (dot(high, fine) + dot(low, own))

    clear()

    def gram0(i, carry):
        @pl.when(i * chunks >= early * loads)
        def _():
            load(i).wait()

        part = at(i, gram_chunk)
        add_gram(xv[part, 0:width], xv[part, width:both])
        return carry

    lax.fori_loop(0, rows // gram_chunk, gram0, 0)

    @pl.when(even)
    def _():
        pl.semaphore_wait(hello.at[0], 1)

    round_start(0)
    exchange(0)
    round_end(0)

    def turn0(i, carry):
        part = at(i, chunk)
        mixed = transform(0, xv[part, 0:width], xv[part, width:both])
        move0[part] = mixed[:, :width]
        stay0[part] = mixed[:, width:]

        @pl.when(jnp.logical_and(i == 3, inner))
        def _():
            skip_move(span(0, ahead)).start()

        @pl.when(jnp.logical_and(i == 3, last))
        def _():
            skip_move(span(0, ahead_last)).start()

        @pl.when(jnp.logical_and(i > early, jnp.logical_not(inner)))
        def _():
            first_move(at(i - 1, chunk), i - 1).start()

        return carry

    lax.fori_loop(0, chunks, turn0, 0)

    if widen > 1:
        round_start(1)

    def start_first(i, carry):
        first_move(at(i, chunk), i).start()
        return carry

    @pl.when(odd)
    def _():
        def start_hold(i, carry):
            hold_move(at(i, chunk), i).start()
            return carry

        lax.fori_loop(early, given_even, start_hold, 0)

    @pl.when(inner)
    def _():
        raw_below(span(0, early), 0).wait_send()
        skip_move(span(ahead, before_first)).start()
        lax.fori_loop(early, chunks, start_first, 0)
        skip_move(span(before_first, after_first)).start()

    @pl.when(last)
    def _():
        start_first(chunks - 1, 0)
        skip_move(span(ahead_last, given_odd)).start()

    @pl.when(even)
    def _():
        start_first(chunks - 1, 0)
        give_move(span(early, given_odd)).start()
        for i in range(early):
            part = span(i, i + 1)
            raw_below(part, i).wait_recv()
            raw_on(part).start()
        skip_move(span(0, given_even)).start()

    mix_below(0)
    raw_next(span(0, early)).wait_recv()
    clear()

    def early0(i, carry):
        part = at(i, chunk)
        mixed = transform(1, raw[part, 0:width], raw[part, width:both])
        come0[part] = mixed[:, :width]
        rest[part] = mixed[:, width:]
        add_gram(mixed[:, :width], stay0[part])
        return carry

    lax.fori_loop(0, early, early0, 0)

    def gram1(i, carry):
        part = at(i, chunk)
        first_move(part, i).wait_recv()

        add_gram(come0[part], stay0[part])
        return carry

    lax.fori_loop(early, chunks, gram1, 0)
    exchange(1)
    for k in range(1, widen):
        if k > 1:
            round_start(k)
        round_end(k)

    def tell(k, carry):
        message(pl.ds(blk, 1), lax.rem(blk + k, blk_count)).start()
        return carry

    lax.fori_loop(1, blk_count, tell, 0)

    def turn1(i, carry):
        part = at(i, chunk)
        mixed = transform(0, come0[part], stay0[part])
        out_ref[part, 0:width] = mixed[:, :width]
        move1[part] = mixed[:, width:]

        @pl.when(jnp.logical_and(i == passing + 1, inner))
        def _():
            hold_move(span(early, given_even), early).wait_send()
            skip_move(span(after_first, given_odd)).start()

        @pl.when(i > passing)
        def _():
            second_move(at(i - 1, chunk)).start()

        return carry

    lax.fori_loop(passing, chunks, turn1, 0)
    second_move(span(chunks - 1, chunks)).start()

    @pl.when(even)
    def _():
        def pass_on(i, carry):
            part = at(i, chunk)
            hold_move(part, i).wait_recv()
            pass_move(part).start()
            return carry

        lax.fori_loop(early, given_even, pass_on, 0)

    def own1(i, carry):
        part = at(i, chunk)
        out_ref[part, 0:width] = transform(0, come0[part], stay0[part])[:, :width]
        return carry

    lax.fori_loop(0, passing, own1, 0)
    mix_below(1)

    @pl.when(odd)
    def _():
        skip_move(span(0, given_odd)).wait_recv()
        give_move(span(early, given_odd)).wait_recv()

    @pl.when(even)
    def _():
        skip_move(span(0, given_even)).wait_recv()
        give_move(span(early, given_even)).wait_recv()

    def early1(i, carry):
        part = at(i, chunk)
        out_ref[part, width:both] = transform(1, skip[part], rest[part])[:, width:]
        return carry

    lax.fori_loop(0, given, early1, 0)

    messages = message(pl.ds(0, blk_count - 1), after)
    messages.wait_recv()
    off_ref[...] = jnp.sum(mgath[...], axis=0) / float(blk_count)

    messages.wait_send()
    first_move(span(early, chunks), early).wait_send()
    for step in range(STEPS):
        cos_move(step).wait_send()

    @pl.when(jnp.logical_not(inner))
    def _():
        raw_next(span(0, early)).wait_send()

    @pl.when(odd)
    def _():
        skip_move(span(0, given_odd)).wait_send()

    @pl.when(last)
    def _():
        hold_move(span(early, given_even), early).wait_send()

    @pl.when(even)
    def _():
        skip_move(span(0, given_even)).wait_send()
        give_move(span(early, given_odd)).wait_send()
        raw_on(span(0, early)).wait_send()
        pass_move(span(early, given_even)).wait_send()

    @pl.when(odd)
    def _():
        second_move(span(given_odd, chunks)).wait_recv()
        second_move(span(given_even, chunks)).wait_send()

    @pl.when(even)
    def _():
        second_move(span(given_even, chunks)).wait_recv()
        second_move(span(given_odd, chunks)).wait_send()


def settle(rotated, off, out_ref, off_ref, scalars, sem):
    whole = pltpu.make_async_copy(rotated, out_ref, sem.at[0])
    whole.start()
    values = off[...]
    lane = lax.broadcasted_iota(jnp.int32, values.shape, 1)
    for step in range(STEPS):
        scalars[step] = jnp.sum(jnp.where(lane == step, values, 0.0))
    few = pltpu.make_async_copy(scalars, off_ref, sem.at[1])
    few.start()
    few.wait()
    whole.wait()


def on_device(row_count, blk_count, matrix):
    rows, both = matrix.shape
    width = both // 2
    chunks, loads, early, given_even, given_odd, _, _ = plan = 16, 4, 3, 8, 7, (2, 3, 5.5), 2.5
    chunk = rows // chunks
    most = max(given_even, given_odd)
    widen = 1
    while 2**widen < blk_count // 2:
        widen += 1
    dma = pltpu.SemaphoreType.DMA
    regular = pltpu.SemaphoreType.REGULAR
    block = pltpu.VMEM((rows, width), F32)
    some = pltpu.VMEM((most * chunk, width), F32)
    few = pltpu.VMEM((early * chunk, both), F32)
    vmem = pl.BlockSpec(memory_space=pltpu.VMEM)
    hbm = pl.BlockSpec(memory_space=pltpu.HBM)
    rotated, off = pl.pallas_call(
        functools.partial(kernel, row_count, blk_count, plan),
        out_shape=(
            jax.ShapeDtypeStruct((rows, both), F32),
            jax.ShapeDtypeStruct((1, width), F32),
        ),
        in_specs=[hbm],
        out_specs=(vmem, vmem),
        scratch_shapes=[
            pltpu.VMEM((rows, both), F32),
            block, block, block, some, block,
            few, few, some, some,
            pltpu.VMEM((both, both), F32),
            pltpu.VMEM((16, width), F32),
            pltpu.VMEM((STEPS, row_count, width + 16, width), F32),
            pltpu.VMEM((2, 2, both, both), BF16),
            pltpu.VMEM((STEPS, width, width), F32),
            pltpu.VMEM((STEPS, width, width), F32),
            pltpu.VMEM((blk_count, 1, width), F32),
            dma((loads,)), dma((early,)), dma((given_even - early,)), dma((chunks - early,)),
            dma((1,)), dma((2 * STEPS,)), dma((8 + STEPS,)), dma((5 + STEPS,)),
            regular((1,)), regular((widen,)), regular((widen,)),
        ],
        compiler_params=pltpu.CompilerParams(
            collective_id=0, has_side_effects=True, vmem_limit_bytes=48 * 1024 * 1024
        ),
    )(matrix)
    return pl.pallas_call(
        settle,
        out_shape=(
            jax.ShapeDtypeStruct((rows, both), F32),
            jax.ShapeDtypeStruct((STEPS,), F32),
        ),
        in_specs=[vmem, vmem],
        out_specs=(hbm, hbm),
        scratch_shapes=[pltpu.SMEM((STEPS,), F32), dma((2,))],
        compiler_params=pltpu.CompilerParams(vmem_limit_bytes=8 * 1024 * 1024),
    )(rotated, off)


def solution(mesh):
    return jax.shard_map(
        functools.partial(on_device, mesh.shape["row"], mesh.shape["blk"]),
        mesh=mesh,
        in_specs=(P("row", "blk"),),
        out_specs=(P("row", "blk"), P()),
        check_vma=False,
    )
```

```python
import functools

import jax
import jax.numpy as jnp
from jax import lax
from jax.experimental import pallas as pl
from jax.experimental.pallas import tpu as pltpu
from jax.sharding import PartitionSpec as P

STEPS = 2
NS_ITERS = 4
MESH = pl.DeviceIdType.MESH
F32 = jnp.float32
BF16 = jnp.bfloat16


def split(value):
    high = value.astype(BF16)
    return high, (value - high.astype(F32)).astype(BF16)


def dot(a, b):
    return jnp.dot(a, b, preferred_element_type=F32)


def product(a, b):
    ah, al = split(a)
    bh, bl = split(b)
    width = b.shape[1]
    both = dot(
        jnp.concatenate([ah, al], axis=1),
        jnp.concatenate(
            [
                jnp.concatenate([bh, bl], axis=1),
                jnp.concatenate([bh, jnp.zeros_like(bl)], axis=1),
            ],
            axis=0,
        ),
    )
    return both[:, :width] + both[:, width:]


def mixing(cosines):
    width = cosines.shape[0]
    rows = lax.broadcasted_iota(jnp.int32, (width, width), 0)
    columns = lax.broadcasted_iota(jnp.int32, (width, width), 1)
    identity = jnp.where(rows == columns, 1.0, 0.0).astype(F32)
    coupling = 0.5 * cosines
    flipped = coupling.T
    scale = 1.0 + jnp.sum(coupling * coupling, keepdims=True)
    shrink = 1.0 / scale
    current = [
        (identity + product(coupling, flipped)) * shrink,
        (identity + product(flipped, coupling)) * shrink,
    ]
    result = [None, None]
    for count in range(NS_ITERS):
        for side in range(2):
            y, z = current[side], result[side]
            inner = y if z is None else product(z, y)
            factor = 1.5 * identity - 0.5 * inner
            if count < NS_ITERS - 1:
                current[side] = product(y, factor)
            result[side] = factor if z is None else product(factor, z)
    root = 1.0 / jnp.sqrt(scale)
    first, second = result[0] * root, result[1] * root
    return (
        jnp.concatenate([first, product(coupling, second)], axis=1),
        jnp.concatenate([-product(flipped, first), second], axis=1),
    )


def kernel(
    row_count, blk_count, plan, x_hbm, out_ref, off_ref,
    xv, move0, stay0, come0, rest, move1, raw, via, skip, hold,
    acc, norms, gath, weights, coses, cosin, mgath,
    load_sem, via_recv, hold_recv, first_recv, row_send, row_recv, send, recv, hello, up, down,
):
    rows, both = x_hbm.shape
    width = both // 2
    chunks, loads, early, given_even, given_odd, pieces, ahead_last = plan
    ahead, before_first, after_first = pieces
    chunk, gram_chunk = rows // chunks, rows // loads
    widen = up.shape[0]
    share = width // row_count
    row, blk = lax.axis_index("row"), lax.axis_index("blk")
    after = lax.rem(blk + 1, blk_count)
    second = lax.rem(blk + 2, blk_count)
    below = lax.rem(blk + blk_count - 1, blk_count)
    odd = lax.rem(blk, 2) == 1
    even = jnp.logical_not(odd)
    last = blk == blk_count - 1
    inner = jnp.logical_and(odd, jnp.logical_not(last))
    passing = jnp.where(odd, given_even, given_odd)
    given = jnp.where(odd, given_odd, given_even)

    barrier = pltpu.get_barrier_semaphore()
    for k in range(1, row_count):
        pl.semaphore_signal(
            barrier, inc=1, device_id={"row": lax.rem(row + k, row_count)}, device_id_type=MESH
        )
    pl.semaphore_signal(barrier, inc=1, device_id={"blk": below}, device_id_type=MESH)

    def at(i, size):
        return pl.ds(pl.multiple_of(i * size, size), size)

    def span(first, last):
        return pl.ds(int(first * chunk), int((last - first) * chunk))

    def load(i):
        return pltpu.make_async_copy(
            x_hbm.at[at(i, gram_chunk)], xv.at[at(i, gram_chunk)], load_sem.at[i]
        )

    def start_load(i, carry):
        load(i).start()
        return carry

    lax.fori_loop(0, rows // gram_chunk, start_load, 0)

    def to_blk(source, target, send, recv, peer):
        return pltpu.make_async_remote_copy(
            src_ref=source, dst_ref=target, send_sem=send, recv_sem=recv,
            device_id={"blk": peer}, device_id_type=MESH,
        )

    RAW, SKIP, REST, SECOND, MEASURE, COS, FIRST, ON = 0, 1, 2, 3, 4, 5, 5 + STEPS, 6 + STEPS
    right = pl.ds(width, width)

    def raw_next(part):
        return to_blk(xv.at[part], raw.at[part], send.at[RAW], recv.at[RAW], after)

    def raw_below(part, i):
        return to_blk(xv.at[part], via.at[part], send.at[RAW], via_recv.at[i], below)

    def raw_on(part):
        return to_blk(via.at[part], raw.at[part], send.at[ON], recv.at[RAW], second)

    def skip_move(part):
        return to_blk(move0.at[part], skip.at[part], send.at[SKIP], recv.at[SKIP], second)

    def first_move(part, i):
        return to_blk(
            move0.at[part], come0.at[part], send.at[FIRST], first_recv.at[i - early], after
        )

    def second_move(part):
        return to_blk(
            move1.at[part], out_ref.at[part, right], send.at[SECOND], recv.at[SECOND], after
        )

    def give_move(part):
        return to_blk(stay0.at[part], rest.at[part], send.at[REST], recv.at[REST], after)

    def hold_move(part, i):
        return to_blk(stay0.at[part], hold.at[part], send.at[REST], hold_recv.at[i - early], below)

    def pass_move(part):
        return to_blk(hold.at[part], rest.at[part], send.at[ON + 1], recv.at[REST], second)

    def cos_move(step):
        part = at(row, share)
        return to_blk(
            coses.at[step, part], cosin.at[step, part], send.at[COS + step], recv.at[COS + step],
            after,
        )

    def cos_copy(step, part, peer):
        return pltpu.make_async_remote_copy(
            src_ref=cosin.at[step, part], dst_ref=cosin.at[step, part],
            send_sem=row_send.at[0], recv_sem=row_recv.at[STEPS + step],
            device_id={"row": peer}, device_id_type=MESH,
        )

    def message(part, peer):
        return to_blk(mgath.at[part], mgath.at[part], send.at[MEASURE], recv.at[MEASURE], peer)

    def tell_in(semaphore, peer):
        pl.semaphore_signal(semaphore, inc=1, device_id={"blk": peer}, device_id_type=MESH)

    def round_start(k):
        tell_in(up.at[k], lax.rem(blk + 2**k, blk_count))
        tell_in(down.at[k], lax.rem(blk + blk_count - 2**k, blk_count))

    def round_end(k):
        pl.semaphore_wait(up.at[k], 1)
        pl.semaphore_wait(down.at[k], 1)

    pl.semaphore_wait(barrier, row_count)
    tell_in(hello.at[0], after)
    for i in range(-(-early * loads // chunks)):
        load(i).wait()

    @pl.when(even)
    def _():
        for i in range(early):
            raw_next(span(i, i + 1)).start()

    @pl.when(odd)
    def _():
        pl.semaphore_wait(hello.at[0], 1)
        for i in range(early):
            raw_below(span(i, i + 1), i).start()

    def add_gram(left, right):
        lh, ll = split(left)
        rh, rl = split(right)
        acc[...] += lax.dot_general(
            jnp.concatenate([lh, ll], axis=1),
            jnp.concatenate([rh, rl], axis=1),
            (((0,), (0,)), ((), ())),
            preferred_element_type=F32,
        )
        norms[0:8] += jnp.sum((left * left).reshape(-1, 8, width), axis=0)
        norms[8:16] += jnp.sum((right * right).reshape(-1, 8, width), axis=0)

    def clear():
        acc[...] = jnp.zeros_like(acc)
        norms[...] = jnp.zeros_like(norms)

    def mix(slot, cosines):
        top, bottom = mixing(cosines)
        high, low = split(top)
        weights[slot, 0, :width] = high
        weights[slot, 1, :width] = low
        high, low = split(bottom)
        weights[slot, 0, width:] = high
        weights[slot, 1, width:] = low

    lane = lax.broadcasted_iota(jnp.int32, (1, width), 1)

    def row_peer(k):
        return lax.rem(row + k, row_count)

    def exchange(step):
        def copy(owners, peer):
            return pltpu.make_async_remote_copy(
                src_ref=gath.at[step, owners], dst_ref=gath.at[step, owners],
                send_sem=row_send.at[0], recv_sem=row_recv.at[step],
                device_id={"row": peer}, device_id_type=MESH,
            )

        gath[step, row, 0:width] = (
            acc[:width, :width] + acc[:width, width:] + acc[width:, :width]
        ) + acc[width:, width:]
        first = jnp.sum(norms[0:8], axis=0, keepdims=True)
        second = jnp.sum(norms[8:16], axis=0, keepdims=True)
        gath[step, row, width:width + 8] = jnp.broadcast_to(first, (8, width))
        gath[step, row, width + 8:width + 16] = jnp.broadcast_to(second, (8, width))
        for k in range(1, row_count):
            copy(pl.ds(row, 1), row_peer(k)).start()
        all_copies = copy(pl.ds(0, row_count - 1), row_peer(1))
        all_copies.wait_recv()
        total = gath[step, 0]
        for r in range(1, row_count):
            total = total + gath[step, r]
        all_copies.wait_send()
        cross = total[:width]
        first = lax.rsqrt(jnp.broadcast_to(total[width:width + 1], (width, width))).T
        second = lax.rsqrt(jnp.broadcast_to(total[width + 8:width + 9], (width, width)))
        cosines = cross * first * second
        coses[step] = cosines
        cos_move(step).start()
        mix(0, cosines)
        summed = jnp.sum(cosines * cosines, keepdims=True)
        own = jnp.where(lane == step, jnp.broadcast_to(summed, (1, width)), 0.0)
        if step == 0:
            mgath[blk] = own
        else:
            mgath[blk] += own

    def mix_below(step):
        cos_move(step).wait_recv()
        for k in range(1, row_count):
            cos_copy(step, at(row, share), row_peer(k)).start()
        all_copies = cos_copy(step, pl.ds(0, (row_count - 1) * share), row_peer(1))
        all_copies.wait_recv()
        mix(1, cosin[step])
        all_copies.wait_send()

    def transform(slot, left, right):
        lh, ll = split(left)
        rh, rl = split(right)
        high = jnp.concatenate([lh, rh], axis=1)
        low = jnp.concatenate([ll, rl], axis=1)
        own, fine = weights[slot, 0], weights[slot, 1]
        return dot(high, own) + (dot(high, fine) + dot(low, own))

    clear()

    def gram0(i, carry):
        @pl.when(i * chunks >= early * loads)
        def _():
            load(i).wait()

        part = at(i, gram_chunk)
        add_gram(xv[part, 0:width], xv[part, width:both])
        return carry

    lax.fori_loop(0, rows // gram_chunk, gram0, 0)

    @pl.when(even)
    def _():
        pl.semaphore_wait(hello.at[0], 1)

    round_start(0)
    exchange(0)
    round_end(0)

    def turn0(i, carry):
        part = at(i, chunk)
        mixed = transform(0, xv[part, 0:width], xv[part, width:both])
        move0[part] = mixed[:, :width]
        stay0[part] = mixed[:, width:]

        @pl.when(jnp.logical_and(i == 3, inner))
        def _():
            skip_move(span(0, ahead)).start()

        @pl.when(jnp.logical_and(i == 3, last))
        def _():
            skip_move(span(0, ahead_last)).start()

        @pl.when(jnp.logical_and(i > early, jnp.logical_not(inner)))
        def _():
            first_move(at(i - 1, chunk), i - 1).start()

        return carry

    lax.fori_loop(0, chunks, turn0, 0)

    if widen > 1:
        round_start(1)

    def start_first(i, carry):
        first_move(at(i, chunk), i).start()
        return carry

    @pl.when(odd)
    def _():
        def start_hold(i, carry):
            hold_move(at(i, chunk), i).start()
            return carry

        lax.fori_loop(early, given_even, start_hold, 0)

    @pl.when(inner)
    def _():
        raw_below(span(0, early), 0).wait_send()
        skip_move(span(ahead, before_first)).start()
        lax.fori_loop(early, chunks, start_first, 0)
        skip_move(span(before_first, after_first)).start()

    @pl.when(last)
    def _():
        start_first(chunks - 1, 0)
        skip_move(span(ahead_last, given_odd)).start()

    @pl.when(even)
    def _():
        start_first(chunks - 1, 0)
        give_move(span(early, given_odd)).start()
        for i in range(early):
            part = span(i, i + 1)
            raw_below(part, i).wait_recv()
            raw_on(part).start()
        skip_move(span(0, given_even)).start()

    mix_below(0)
    raw_next(span(0, early)).wait_recv()
    clear()

    def early0(i, carry):
        part = at(i, chunk)
        mixed = transform(1, raw[part, 0:width], raw[part, width:both])
        come0[part] = mixed[:, :width]
        rest[part] = mixed[:, width:]
        add_gram(mixed[:, :width], stay0[part])
        return carry

    lax.fori_loop(0, early, early0, 0)

    def gram1(i, carry):
        part = at(i, chunk)
        first_move(part, i).wait_recv()

        add_gram(come0[part], stay0[part])
        return carry

    lax.fori_loop(early, chunks, gram1, 0)
    def pass_rest(start, stop):
        def pass_on(i, carry):
            part = at(i, chunk)
            hold_move(part, i).wait_recv()
            pass_move(part).start()
            return carry

        @pl.when(even)
        def _():
            lax.fori_loop(early + start, early + stop, pass_on, 0)

    pass_rest(0, 1)
    exchange(1)
    pass_rest(1, 2)
    for k in range(1, widen):
        if k > 1:
            round_start(k)
        round_end(k)

    def tell(k, carry):
        message(pl.ds(blk, 1), lax.rem(blk + k, blk_count)).start()
        return carry

    lax.fori_loop(1, blk_count, tell, 0)

    def turn1(i, carry):
        part = at(i, chunk)
        mixed = transform(0, come0[part], stay0[part])
        out_ref[part, 0:width] = mixed[:, :width]
        move1[part] = mixed[:, width:]

        @pl.when(jnp.logical_and(i == passing + 1, inner))
        def _():
            hold_move(span(early, given_even), early).wait_send()
            skip_move(span(after_first, given_odd)).start()

        @pl.when(i > passing)
        def _():
            second_move(at(i - 1, chunk)).start()

        return carry

    lax.fori_loop(passing, chunks, turn1, 0)
    second_move(span(chunks - 1, chunks)).start()

    pass_rest(2, given_even - early)

    def own1(i, carry):
        part = at(i, chunk)
        out_ref[part, 0:width] = transform(0, come0[part], stay0[part])[:, :width]
        return carry

    lax.fori_loop(0, passing, own1, 0)
    mix_below(1)

    @pl.when(odd)
    def _():
        skip_move(span(0, given_odd)).wait_recv()
        give_move(span(early, given_odd)).wait_recv()

    @pl.when(even)
    def _():
        skip_move(span(0, given_even)).wait_recv()
        give_move(span(early, given_even)).wait_recv()

    def early1(i, carry):
        part = at(i, chunk)
        out_ref[part, width:both] = transform(1, skip[part], rest[part])[:, width:]
        return carry

    lax.fori_loop(0, given, early1, 0)

    messages = message(pl.ds(0, blk_count - 1), after)
    messages.wait_recv()
    off_ref[...] = jnp.sum(mgath[...], axis=0) / float(blk_count)

    messages.wait_send()
    first_move(span(early, chunks), early).wait_send()
    for step in range(STEPS):
        cos_move(step).wait_send()

    @pl.when(jnp.logical_not(inner))
    def _():
        raw_next(span(0, early)).wait_send()

    @pl.when(odd)
    def _():
        skip_move(span(0, given_odd)).wait_send()

    @pl.when(last)
    def _():
        hold_move(span(early, given_even), early).wait_send()

    @pl.when(even)
    def _():
        skip_move(span(0, given_even)).wait_send()
        give_move(span(early, given_odd)).wait_send()
        raw_on(span(0, early)).wait_send()
        pass_move(span(early, given_even)).wait_send()

    @pl.when(odd)
    def _():
        second_move(span(given_odd, chunks)).wait_recv()
        second_move(span(given_even, chunks)).wait_send()

    @pl.when(even)
    def _():
        second_move(span(given_even, chunks)).wait_recv()
        second_move(span(given_odd, chunks)).wait_send()


def settle(rotated, off, out_ref, off_ref, scalars, sem):
    whole = pltpu.make_async_copy(rotated, out_ref, sem.at[0])
    whole.start()
    values = off[...]
    lane = lax.broadcasted_iota(jnp.int32, values.shape, 1)
    for step in range(STEPS):
        scalars[step] = jnp.sum(jnp.where(lane == step, values, 0.0))
    few = pltpu.make_async_copy(scalars, off_ref, sem.at[1])
    few.start()
    few.wait()
    whole.wait()


def on_device(row_count, blk_count, matrix):
    rows, both = matrix.shape
    width = both // 2
    chunks, loads, early, given_even, given_odd, _, _ = plan = 16, 4, 3, 9, 8, (2, 3, 7.25), 2.5
    chunk = rows // chunks
    most = max(given_even, given_odd)
    widen = 1
    while 2**widen < blk_count // 2:
        widen += 1
    dma = pltpu.SemaphoreType.DMA
    regular = pltpu.SemaphoreType.REGULAR
    block = pltpu.VMEM((rows, width), F32)
    some = pltpu.VMEM((most * chunk, width), F32)
    few = pltpu.VMEM((early * chunk, both), F32)
    vmem = pl.BlockSpec(memory_space=pltpu.VMEM)
    hbm = pl.BlockSpec(memory_space=pltpu.HBM)
    rotated, off = pl.pallas_call(
        functools.partial(kernel, row_count, blk_count, plan),
        out_shape=(
            jax.ShapeDtypeStruct((rows, both), F32),
            jax.ShapeDtypeStruct((1, width), F32),
        ),
        in_specs=[hbm],
        out_specs=(vmem, vmem),
        scratch_shapes=[
            pltpu.VMEM((rows, both), F32),
            block, block, block, some, block,
            few, few, some, some,
            pltpu.VMEM((both, both), F32),
            pltpu.VMEM((16, width), F32),
            pltpu.VMEM((STEPS, row_count, width + 16, width), F32),
            pltpu.VMEM((2, 2, both, both), BF16),
            pltpu.VMEM((STEPS, width, width), F32),
            pltpu.VMEM((STEPS, width, width), F32),
            pltpu.VMEM((blk_count, 1, width), F32),
            dma((loads,)), dma((early,)), dma((given_even - early,)), dma((chunks - early,)),
            dma((1,)), dma((2 * STEPS,)), dma((8 + STEPS,)), dma((5 + STEPS,)),
            regular((1,)), regular((widen,)), regular((widen,)),
        ],
        compiler_params=pltpu.CompilerParams(
            collective_id=0, has_side_effects=True, vmem_limit_bytes=48 * 1024 * 1024
        ),
    )(matrix)
    return pl.pallas_call(
        settle,
        out_shape=(
            jax.ShapeDtypeStruct((rows, both), F32),
            jax.ShapeDtypeStruct((STEPS,), F32),
        ),
        in_specs=[vmem, vmem],
        out_specs=(hbm, hbm),
        scratch_shapes=[pltpu.SMEM((STEPS,), F32), dma((2,))],
        compiler_params=pltpu.CompilerParams(vmem_limit_bytes=8 * 1024 * 1024),
    )(rotated, off)


def solution(mesh):
    return jax.shard_map(
        functools.partial(on_device, mesh.shape["row"], mesh.shape["blk"]),
        mesh=mesh,
        in_specs=(P("row", "blk"),),
        out_specs=(P("row", "blk"), P()),
        check_vma=False,
    )
```

```python
import functools
import math

import jax
import jax.numpy as jnp
from jax import lax
from jax.experimental import pallas as pl
from jax.experimental.pallas import tpu as pltpu
from jax.sharding import PartitionSpec as P

STEPS = 2
NS_ITERS = 4
MESH = pl.DeviceIdType.MESH
F32 = jnp.float32
BF16 = jnp.bfloat16


def split(value):
    high = value.astype(BF16)
    return high, (value - high.astype(F32)).astype(BF16)


def dot(a, b):
    return jnp.dot(a, b, preferred_element_type=F32)


def product(a, b):
    ah, al = split(a)
    bh, bl = split(b)
    width = b.shape[1]
    both = dot(
        jnp.concatenate([ah, al], axis=1),
        jnp.concatenate(
            [
                jnp.concatenate([bh, bl], axis=1),
                jnp.concatenate([bh, jnp.zeros_like(bl)], axis=1),
            ],
            axis=0,
        ),
    )
    return both[:, :width] + both[:, width:]


def mixing(cosines):
    width = cosines.shape[0]
    rows = lax.broadcasted_iota(jnp.int32, (width, width), 0)
    columns = lax.broadcasted_iota(jnp.int32, (width, width), 1)
    identity = jnp.where(rows == columns, 1.0, 0.0).astype(F32)
    coupling = 0.5 * cosines
    flipped = coupling.T
    scale = 1.0 + jnp.sum(coupling * coupling, keepdims=True)
    shrink = 1.0 / scale
    current = [
        (identity + product(coupling, flipped)) * shrink,
        (identity + product(flipped, coupling)) * shrink,
    ]
    result = [None, None]
    for count in range(NS_ITERS):
        for side in range(2):
            y, z = current[side], result[side]
            inner = y if z is None else product(z, y)
            factor = 1.5 * identity - 0.5 * inner
            if count < NS_ITERS - 1:
                current[side] = product(y, factor)
            result[side] = factor if z is None else product(factor, z)
    root = 1.0 / jnp.sqrt(scale)
    first, second = result[0] * root, result[1] * root
    return (
        jnp.concatenate([first, product(coupling, second)], axis=1),
        jnp.concatenate([-product(flipped, first), second], axis=1),
    )


def kernel(
    row_count, blk_count, plan, x_hbm, out_ref, off_ref,
    xv, move0, stay0, come0, rest, move1, raw, via, skip, hold,
    acc, norms, gath, weights, coses, cosin, mgath,
    load_sem, via_recv, hold_recv, first_recv, row_send, row_recv, send, recv, hello, up, down,
):
    rows, both = x_hbm.shape
    width = both // 2
    chunks, loads, early, given, pieces, ahead_last = plan
    ahead, before_first, after_first = pieces
    chunk, gram_chunk = rows // chunks, rows // loads
    widen = up.shape[0]
    share = width // row_count
    row, blk = lax.axis_index("row"), lax.axis_index("blk")
    after = lax.rem(blk + 1, blk_count)
    second = lax.rem(blk + 2, blk_count)
    below = lax.rem(blk + blk_count - 1, blk_count)
    odd = lax.rem(blk, 2) == 1
    even = jnp.logical_not(odd)
    last = blk == blk_count - 1
    inner = jnp.logical_and(odd, jnp.logical_not(last))

    def each(target):
        others, parity = target > 2, lax.rem(target, 2)
        return [
            (given[0], target == 0),
            (given[1], target == 1),
            (given[2], target == 2),
            (given[3], jnp.logical_and(others, parity == 0)),
            (given[4], jnp.logical_and(others, parity == 1)),
        ]

    def whole_chunks(target):
        count = jnp.int32(0)
        for amount, chosen in each(target):
            count = jnp.where(chosen, jnp.int32(int(amount)), count)
        return count

    def for_each(target, act, also=None, kinds=range(5)):
        for kind in kinds:
            amount, chosen = each(target)[kind]
            pl.when(chosen if also is None else jnp.logical_and(chosen, also))(
                functools.partial(act, amount)
            )

    passing, own_given = whole_chunks(after), whole_chunks(blk)

    barrier = pltpu.get_barrier_semaphore()
    pl.semaphore_signal(barrier, inc=1, device_id={"blk": below}, device_id_type=MESH)

    def tell_row(semaphore):
        for k in range(1, row_count):
            pl.semaphore_signal(
                semaphore, inc=1, device_id={"row": lax.rem(row + k, row_count)},
                device_id_type=MESH,
            )

    @pl.when(odd)
    def _():
        tell_row(barrier)

    def at(i, size):
        return pl.ds(pl.multiple_of(i * size, size), size)

    def span(first, last):
        return pl.ds(int(first * chunk), int((last - first) * chunk))

    def load(i):
        return pltpu.make_async_copy(
            x_hbm.at[at(i, gram_chunk)], xv.at[at(i, gram_chunk)], load_sem.at[i]
        )

    def start_load(i, carry):
        load(i).start()
        return carry

    lax.fori_loop(0, rows // gram_chunk, start_load, 0)

    def to_blk(source, target, send, recv, peer):
        return pltpu.make_async_remote_copy(
            src_ref=source, dst_ref=target, send_sem=send, recv_sem=recv,
            device_id={"blk": peer}, device_id_type=MESH,
        )

    RAW, SKIP, REST, SECOND, MEASURE, COS, FIRST, ON = 0, 1, 2, 3, 4, 5, 5 + STEPS, 6 + STEPS
    right = pl.ds(width, width)

    def raw_next(part):
        return to_blk(xv.at[part], raw.at[part], send.at[RAW], recv.at[RAW], after)

    def raw_below(part, i):
        return to_blk(xv.at[part], via.at[part], send.at[RAW], via_recv.at[i], below)

    def raw_on(part):
        return to_blk(via.at[part], raw.at[part], send.at[ON], recv.at[RAW], second)

    def skip_move(part):
        return to_blk(move0.at[part], skip.at[part], send.at[SKIP], recv.at[SKIP], second)

    def first_move(part, i):
        return to_blk(
            move0.at[part], come0.at[part], send.at[FIRST], first_recv.at[i - early], after
        )

    def second_move(part):
        return to_blk(
            move1.at[part], out_ref.at[part, right], send.at[SECOND], recv.at[SECOND], after
        )

    def give_move(part):
        return to_blk(stay0.at[part], rest.at[part], send.at[REST], recv.at[REST], after)

    def hold_move(part, i):
        return to_blk(stay0.at[part], hold.at[part], send.at[REST], hold_recv.at[i - early], below)

    def pass_move(part):
        return to_blk(hold.at[part], rest.at[part], send.at[ON + 1], recv.at[REST], second)

    def cos_move(step):
        part = at(row, share)
        return to_blk(
            coses.at[step, part], cosin.at[step, part], send.at[COS + step], recv.at[COS + step],
            after,
        )

    def cos_copy(step, part, peer):
        return pltpu.make_async_remote_copy(
            src_ref=cosin.at[step, part], dst_ref=cosin.at[step, part],
            send_sem=row_send.at[0], recv_sem=row_recv.at[STEPS + step],
            device_id={"row": peer}, device_id_type=MESH,
        )

    def message(part, peer):
        return to_blk(mgath.at[part], mgath.at[part], send.at[MEASURE], recv.at[MEASURE], peer)

    def tell_in(semaphore, peer):
        pl.semaphore_signal(semaphore, inc=1, device_id={"blk": peer}, device_id_type=MESH)

    def round_start(k):
        tell_in(up.at[k], lax.rem(blk + 2**k, blk_count))
        tell_in(down.at[k], lax.rem(blk + blk_count - 2**k, blk_count))

    def round_end(k):
        pl.semaphore_wait(up.at[k], 1)
        pl.semaphore_wait(down.at[k], 1)

    def first_loads():
        for i in range(-(-early * loads // chunks)):
            load(i).wait()

    @pl.when(even)
    def _():
        pl.semaphore_wait(barrier, 1)
        tell_in(hello.at[0], after)
        first_loads()
        for i in range(early):
            raw_next(span(i, i + 1)).start()

    @pl.when(odd)
    def _():
        first_loads()
        pl.semaphore_wait(hello.at[0], 1)
        for i in range(early):
            raw_below(span(i, i + 1), i).start()
        pl.semaphore_wait(barrier, row_count)
        tell_in(hello.at[0], after)
        tell_row(hello.at[1])

    def add_gram(left, right):
        lh, ll = split(left)
        rh, rl = split(right)
        acc[...] += lax.dot_general(
            jnp.concatenate([lh, ll], axis=1),
            jnp.concatenate([rh, rl], axis=1),
            (((0,), (0,)), ((), ())),
            preferred_element_type=F32,
        )
        norms[0:8] += jnp.sum((left * left).reshape(-1, 8, width), axis=0)
        norms[8:16] += jnp.sum((right * right).reshape(-1, 8, width), axis=0)

    def clear():
        acc[...] = jnp.zeros_like(acc)
        norms[...] = jnp.zeros_like(norms)

    def mix(slot, cosines):
        top, bottom = mixing(cosines)
        high, low = split(top)
        weights[slot, 0, :width] = high
        weights[slot, 1, :width] = low
        high, low = split(bottom)
        weights[slot, 0, width:] = high
        weights[slot, 1, width:] = low

    lane = lax.broadcasted_iota(jnp.int32, (1, width), 1)

    def row_peer(k):
        return lax.rem(row + k, row_count)

    def exchange(step):
        def copy(owners, peer):
            return pltpu.make_async_remote_copy(
                src_ref=gath.at[step, owners], dst_ref=gath.at[step, owners],
                send_sem=row_send.at[0], recv_sem=row_recv.at[step],
                device_id={"row": peer}, device_id_type=MESH,
            )

        gath[step, row, 0:width] = (
            acc[:width, :width] + acc[:width, width:] + acc[width:, :width]
        ) + acc[width:, width:]
        first = jnp.sum(norms[0:8], axis=0, keepdims=True)
        second = jnp.sum(norms[8:16], axis=0, keepdims=True)
        gath[step, row, width:width + 8] = jnp.broadcast_to(first, (8, width))
        gath[step, row, width + 8:width + 16] = jnp.broadcast_to(second, (8, width))
        for k in range(1, row_count):
            copy(pl.ds(row, 1), row_peer(k)).start()
        all_copies = copy(pl.ds(0, row_count - 1), row_peer(1))
        all_copies.wait_recv()
        total = gath[step, 0]
        for r in range(1, row_count):
            total = total + gath[step, r]
        all_copies.wait_send()
        cross = total[:width]
        first = lax.rsqrt(jnp.broadcast_to(total[width:width + 1], (width, width))).T
        second = lax.rsqrt(jnp.broadcast_to(total[width + 8:width + 9], (width, width)))
        cosines = cross * first * second
        coses[step] = cosines
        cos_move(step).start()
        mix(0, cosines)
        summed = jnp.sum(cosines * cosines, keepdims=True)
        own = jnp.where(lane == step, jnp.broadcast_to(summed, (1, width)), 0.0)
        if step == 0:
            mgath[blk] = own
        else:
            mgath[blk] += own

    def mix_below(step):
        cos_move(step).wait_recv()
        for k in range(1, row_count):
            cos_copy(step, at(row, share), row_peer(k)).start()
        all_copies = cos_copy(step, pl.ds(0, (row_count - 1) * share), row_peer(1))
        all_copies.wait_recv()
        mix(1, cosin[step])
        all_copies.wait_send()

    def transform(slot, left, right):
        lh, ll = split(left)
        rh, rl = split(right)
        high = jnp.concatenate([lh, rh], axis=1)
        low = jnp.concatenate([ll, rl], axis=1)
        own, fine = weights[slot, 0], weights[slot, 1]
        return dot(high, own) + (dot(high, fine) + dot(low, own))

    clear()

    def gram0(i, carry):
        @pl.when(i * chunks >= early * loads)
        def _():
            load(i).wait()

        part = at(i, gram_chunk)
        add_gram(xv[part, 0:width], xv[part, width:both])
        return carry

    lax.fori_loop(0, rows // gram_chunk, gram0, 0)

    @pl.when(odd)
    def _():
        pl.semaphore_wait(hello.at[1], row_count - 1)
        tell_in(hello.at[1], below)

    @pl.when(even)
    def _():
        pl.semaphore_wait(hello.at[0], 1)
        pl.semaphore_wait(hello.at[1], 1)

    round_start(0)
    exchange(0)
    round_end(0)

    def turn0(i, carry):
        part = at(i, chunk)
        mixed = transform(0, xv[part, 0:width], xv[part, width:both])
        move0[part] = mixed[:, :width]
        stay0[part] = mixed[:, width:]

        @pl.when(jnp.logical_and(i == 3, inner))
        def _():
            skip_move(span(0, ahead)).start()

        @pl.when(jnp.logical_and(i == 3, last))
        def _():
            skip_move(span(0, ahead_last)).start()

        @pl.when(jnp.logical_and(i > early, jnp.logical_not(inner)))
        def _():
            first_move(at(i - 1, chunk), i - 1).start()

        return carry

    lax.fori_loop(0, chunks, turn0, 0)

    if widen > 1:
        round_start(1)

    def start_first(i, carry):
        first_move(at(i, chunk), i).start()
        return carry

    def start_hold(i, carry):
        hold_move(at(i, chunk), i).start()
        return carry

    @pl.when(odd)
    def _():
        lax.fori_loop(early, passing, start_hold, 0)

    def start_hold_end(amount):
        if amount > int(amount):
            hold_move(span(int(amount), amount), int(amount)).start()

    for_each(after, start_hold_end, odd)

    @pl.when(inner)
    def _():
        raw_below(span(0, early), 0).wait_send()
        tell_row(hello.at[2])
        pl.semaphore_wait(hello.at[2], row_count - 1)
        skip_move(span(ahead, before_first)).start()
        lax.fori_loop(early, chunks, start_first, 0)

    def skip_between(amount):
        skip_move(span(before_first, after_first - given[3] + amount)).start()

    for_each(after, skip_between, inner, (2, 3))

    @pl.when(last)
    def _():
        start_first(chunks - 1, 0)
        skip_move(span(ahead_last, given[1])).start()

    @pl.when(even)
    def _():
        start_first(chunks - 1, 0)

    def give(amount):
        give_move(span(early, amount)).start()

    for_each(after, give, even)

    @pl.when(even)
    def _():
        for i in range(early):
            part = span(i, i + 1)
            raw_below(part, i).wait_recv()
            raw_on(part).start()

    def skip_all(amount):
        skip_move(span(0, amount)).start()

    for_each(second, skip_all, even)

    mix_below(0)
    raw_next(span(0, early)).wait_recv()
    clear()

    def early0(i, carry):
        part = at(i, chunk)
        mixed = transform(1, raw[part, 0:width], raw[part, width:both])
        come0[part] = mixed[:, :width]
        rest[part] = mixed[:, width:]
        add_gram(mixed[:, :width], stay0[part])
        return carry

    lax.fori_loop(0, early, early0, 0)

    def gram1(i, carry):
        part = at(i, chunk)
        first_move(part, i).wait_recv()

        add_gram(come0[part], stay0[part])
        return carry

    lax.fori_loop(early, chunks, gram1, 0)
    def pass_rest(start, stop):
        def pass_on(i, carry):
            part = at(i, chunk)
            hold_move(part, i).wait_recv()
            pass_move(part).start()
            return carry

        @pl.when(even)
        def _():
            lax.fori_loop(early + start, stop, pass_on, 0)

    def pass_end(amount):
        if amount > int(amount):
            part = span(int(amount), amount)
            hold_move(part, int(amount)).wait_recv()
            pass_move(part).start()

    pass_rest(0, early + 1)
    exchange(1)
    pass_rest(1, early + 2)
    for k in range(1, widen):
        if k > 1:
            round_start(k)
        round_end(k)

    def tell(k, carry):
        message(pl.ds(blk, 1), lax.rem(blk + k, blk_count)).start()
        return carry

    lax.fori_loop(1, blk_count, tell, 0)

    def hold_sent(amount):
        hold_move(span(early, amount), early).wait_send()

    def turn1(i, carry):
        part = at(i, chunk)
        mixed = transform(0, come0[part], stay0[part])
        out_ref[part, 0:width] = mixed[:, :width]
        move1[part] = mixed[:, width:]

        @pl.when(jnp.logical_and(i == passing + 1, inner))
        def _():
            for_each(after, hold_sent)

        def skip_end(amount):
            skip_move(span(after_first - given[3] + amount, given[4])).start()

        for_each(after, skip_end, jnp.logical_and(i == passing + 1, inner), (2, 3))

        def begin_second(amount):
            second_move(span(amount, int(amount) + 1)).start()

        for_each(after, begin_second, i == passing + 1)

        @pl.when(i > passing + 1)
        def _():
            second_move(at(i - 1, chunk)).start()

        return carry

    lax.fori_loop(passing, chunks, turn1, 0)
    second_move(span(chunks - 1, chunks)).start()

    pass_rest(2, whole_chunks(second))
    for_each(second, pass_end, even)

    def own1(i, carry):
        part = at(i, chunk)
        out_ref[part, 0:width] = transform(0, come0[part], stay0[part])[:, :width]
        return carry

    lax.fori_loop(0, passing, own1, 0)
    mix_below(1)

    def skip_rest_wait(amount):
        skip_move(span(0, amount)).wait_recv()
        give_move(span(early, amount)).wait_recv()

    for_each(blk, skip_rest_wait)

    def finish_part(part):
        out_ref[part, width:both] = transform(1, skip[part], rest[part])[:, width:]

    def early1(i, carry):
        finish_part(at(i, chunk))
        return carry

    lax.fori_loop(0, own_given, early1, 0)

    def early1_end(amount):
        if amount > int(amount):
            finish_part(span(int(amount), amount))

    for_each(blk, early1_end)
    messages = message(pl.ds(0, blk_count - 1), after)
    messages.wait_recv()
    off_ref[...] = jnp.sum(mgath[...], axis=0) / float(blk_count)

    messages.wait_send()
    first_move(span(early, chunks), early).wait_send()
    for step in range(STEPS):
        cos_move(step).wait_send()

    @pl.when(jnp.logical_not(inner))
    def _():
        raw_next(span(0, early)).wait_send()

    def skip_sent(amount):
        skip_move(span(0, amount)).wait_send()

    for_each(second, skip_sent)

    for_each(after, hold_sent, last)

    @pl.when(even)
    def _():
        raw_on(span(0, early)).wait_send()

    def give_sent(amount):
        give_move(span(early, amount)).wait_send()

    for_each(after, give_sent, even)

    def pass_sent(amount):
        pass_move(span(early, amount)).wait_send()

    for_each(second, pass_sent, even)

    def second_sent(amount):
        second_move(span(amount, chunks)).wait_send()

    for_each(after, second_sent)

    def second_arrived(amount):
        second_move(span(amount, chunks)).wait_recv()

    for_each(blk, second_arrived)


def settle(rotated, off, out_ref, off_ref, scalars, sem):
    whole = pltpu.make_async_copy(rotated, out_ref, sem.at[0])
    whole.start()
    values = off[...]
    lane = lax.broadcasted_iota(jnp.int32, values.shape, 1)
    for step in range(STEPS):
        scalars[step] = jnp.sum(jnp.where(lane == step, values, 0.0))
    few = pltpu.make_async_copy(scalars, off_ref, sem.at[1])
    few.start()
    few.wait()
    whole.wait()


def on_device(row_count, blk_count, matrix):
    rows, both = matrix.shape
    width = both // 2
    chunks, loads, early, given, _, _ = plan = 16, 4, 3, (9, 7.5, 8.625, 9, 8), (3, 3.25, 7.5), 2.5
    chunk = rows // chunks
    most = math.ceil(max(given))
    widen = 1
    while 2**widen < blk_count // 2:
        widen += 1
    dma = pltpu.SemaphoreType.DMA
    regular = pltpu.SemaphoreType.REGULAR
    block = pltpu.VMEM((rows, width), F32)
    some = pltpu.VMEM((most * chunk, width), F32)
    few = pltpu.VMEM((early * chunk, both), F32)
    vmem = pl.BlockSpec(memory_space=pltpu.VMEM)
    hbm = pl.BlockSpec(memory_space=pltpu.HBM)
    rotated, off = pl.pallas_call(
        functools.partial(kernel, row_count, blk_count, plan),
        out_shape=(
            jax.ShapeDtypeStruct((rows, both), F32),
            jax.ShapeDtypeStruct((1, width), F32),
        ),
        in_specs=[hbm],
        out_specs=(vmem, vmem),
        scratch_shapes=[
            pltpu.VMEM((rows, both), F32),
            block, block, block, some, block,
            few, few, some, some,
            pltpu.VMEM((both, both), F32),
            pltpu.VMEM((16, width), F32),
            pltpu.VMEM((STEPS, row_count, width + 16, width), F32),
            pltpu.VMEM((2, 2, both, both), BF16),
            pltpu.VMEM((STEPS, width, width), F32),
            pltpu.VMEM((STEPS, width, width), F32),
            pltpu.VMEM((blk_count, 1, width), F32),
            dma((loads,)), dma((early,)), dma((most - early,)), dma((chunks - early,)),
            dma((1,)), dma((2 * STEPS,)), dma((8 + STEPS,)), dma((5 + STEPS,)),
            regular((3,)), regular((widen,)), regular((widen,)),
        ],
        compiler_params=pltpu.CompilerParams(
            collective_id=0, has_side_effects=True, vmem_limit_bytes=48 * 1024 * 1024
        ),
    )(matrix)
    return pl.pallas_call(
        settle,
        out_shape=(
            jax.ShapeDtypeStruct((rows, both), F32),
            jax.ShapeDtypeStruct((STEPS,), F32),
        ),
        in_specs=[vmem, vmem],
        out_specs=(hbm, hbm),
        scratch_shapes=[pltpu.SMEM((STEPS,), F32), dma((2,))],
        compiler_params=pltpu.CompilerParams(vmem_limit_bytes=8 * 1024 * 1024),
    )(rotated, off)


def solution(mesh):
    return jax.shard_map(
        functools.partial(on_device, mesh.shape["row"], mesh.shape["blk"]),
        mesh=mesh,
        in_specs=(P("row", "blk"),),
        out_specs=(P("row", "blk"), P()),
        check_vma=False,
    )
```

```python
import functools
import math

import jax
import jax.numpy as jnp
from jax import lax
from jax.experimental import pallas as pl
from jax.experimental.pallas import tpu as pltpu
from jax.sharding import PartitionSpec as P

STEPS = 2
NS_ITERS = 4
MESH = pl.DeviceIdType.MESH
F32 = jnp.float32
BF16 = jnp.bfloat16


def split(value):
    high = value.astype(BF16)
    return high, (value - high.astype(F32)).astype(BF16)


def dot(a, b):
    return jnp.dot(a, b, preferred_element_type=F32)


def product(a, b):
    ah, al = split(a)
    bh, bl = split(b)
    width = b.shape[1]
    both = dot(
        jnp.concatenate([ah, al], axis=1),
        jnp.concatenate(
            [
                jnp.concatenate([bh, bl], axis=1),
                jnp.concatenate([bh, jnp.zeros_like(bl)], axis=1),
            ],
            axis=0,
        ),
    )
    return both[:, :width] + both[:, width:]


def mixing(cosines):
    width = cosines.shape[0]
    rows = lax.broadcasted_iota(jnp.int32, (width, width), 0)
    columns = lax.broadcasted_iota(jnp.int32, (width, width), 1)
    identity = jnp.where(rows == columns, 1.0, 0.0).astype(F32)
    coupling = 0.5 * cosines
    flipped = coupling.T
    scale = 1.0 + jnp.sum(coupling * coupling, keepdims=True)
    shrink = 1.0 / scale
    current = [
        (identity + product(coupling, flipped)) * shrink,
        (identity + product(flipped, coupling)) * shrink,
    ]
    result = [None, None]
    for count in range(NS_ITERS):
        for side in range(2):
            y, z = current[side], result[side]
            inner = y if z is None else product(z, y)
            factor = 1.5 * identity - 0.5 * inner
            if count < NS_ITERS - 1:
                current[side] = product(y, factor)
            result[side] = factor if z is None else product(factor, z)
    root = 1.0 / jnp.sqrt(scale)
    first, second = result[0] * root, result[1] * root
    return (
        jnp.concatenate([first, product(coupling, second)], axis=1),
        jnp.concatenate([-product(flipped, first), second], axis=1),
    )


def kernel(
    row_count, blk_count, plan, x_hbm, out_ref, off_ref,
    xv, move0, stay0, come0, rest, move1, raw, via, skip, hold,
    acc, norms, gath, weights, coses, cosin, mgath,
    load_sem, via_recv, hold_recv, first_recv, row_send, row_recv, send, recv, hello, up, down,
):
    rows, both = x_hbm.shape
    width = both // 2
    chunks, loads, early, given, pieces, ahead_last = plan
    ahead, before_first, after_first = pieces
    chunk, gram_chunk = rows // chunks, rows // loads
    widen = up.shape[0]
    share = width // row_count
    row, blk = lax.axis_index("row"), lax.axis_index("blk")
    after = lax.rem(blk + 1, blk_count)
    second = lax.rem(blk + 2, blk_count)
    below = lax.rem(blk + blk_count - 1, blk_count)
    odd = lax.rem(blk, 2) == 1
    even = jnp.logical_not(odd)
    last = blk == blk_count - 1
    inner = jnp.logical_and(odd, jnp.logical_not(last))

    def each(target):
        others, parity = target > 2, lax.rem(target, 2)
        return [
            (given[0], target == 0),
            (given[1], target == 1),
            (given[2], target == 2),
            (given[3], jnp.logical_and(others, parity == 0)),
            (given[4], jnp.logical_and(others, parity == 1)),
        ]

    def whole_chunks(target):
        count = jnp.int32(0)
        for amount, chosen in each(target):
            count = jnp.where(chosen, jnp.int32(int(amount)), count)
        return count

    def for_each(target, act, also=None, kinds=range(5)):
        for kind in kinds:
            amount, chosen = each(target)[kind]
            pl.when(chosen if also is None else jnp.logical_and(chosen, also))(
                functools.partial(act, amount)
            )

    passing, own_given = whole_chunks(after), whole_chunks(blk)

    barrier = pltpu.get_barrier_semaphore()
    pl.semaphore_signal(barrier, inc=1, device_id={"blk": below}, device_id_type=MESH)

    def tell_row(semaphore):
        for k in range(1, row_count):
            pl.semaphore_signal(
                semaphore, inc=1, device_id={"row": lax.rem(row + k, row_count)},
                device_id_type=MESH,
            )

    @pl.when(odd)
    def _():
        tell_row(barrier)

    def at(i, size):
        return pl.ds(pl.multiple_of(i * size, size), size)

    def span(first, last):
        return pl.ds(int(first * chunk), int((last - first) * chunk))

    def load(i):
        return pltpu.make_async_copy(
            x_hbm.at[at(i, gram_chunk)], xv.at[at(i, gram_chunk)], load_sem.at[i]
        )

    def start_load(i, carry):
        load(i).start()
        return carry

    lax.fori_loop(0, rows // gram_chunk, start_load, 0)

    def to_blk(source, target, send, recv, peer):
        return pltpu.make_async_remote_copy(
            src_ref=source, dst_ref=target, send_sem=send, recv_sem=recv,
            device_id={"blk": peer}, device_id_type=MESH,
        )

    RAW, SKIP, REST, SECOND, MEASURE, COS, FIRST, ON = 0, 1, 2, 3, 4, 5, 5 + STEPS, 6 + STEPS
    right = pl.ds(width, width)

    def raw_next(part):
        return to_blk(xv.at[part], raw.at[part], send.at[RAW], recv.at[RAW], after)

    def raw_below(part, i):
        return to_blk(xv.at[part], via.at[part], send.at[RAW], via_recv.at[i], below)

    def raw_on(part):
        return to_blk(via.at[part], raw.at[part], send.at[ON], recv.at[RAW], second)

    def skip_move(part):
        return to_blk(move0.at[part], skip.at[part], send.at[SKIP], recv.at[SKIP], second)

    def first_move(part, i):
        return to_blk(
            move0.at[part], come0.at[part], send.at[FIRST], first_recv.at[i - early], after
        )

    def second_move(part):
        return to_blk(
            move1.at[part], out_ref.at[part, right], send.at[SECOND], recv.at[SECOND], after
        )

    def give_move(part):
        return to_blk(stay0.at[part], rest.at[part], send.at[REST], recv.at[REST], after)

    def hold_move(part, i):
        return to_blk(stay0.at[part], hold.at[part], send.at[REST], hold_recv.at[i - early], below)

    def pass_move(part):
        return to_blk(hold.at[part], rest.at[part], send.at[ON + 1], recv.at[REST], second)

    def cos_move(step):
        part = at(row, share)
        return to_blk(
            coses.at[step, part], cosin.at[step, part], send.at[COS + step], recv.at[COS + step],
            after,
        )

    def cos_copy(step, part, peer):
        return pltpu.make_async_remote_copy(
            src_ref=cosin.at[step, part], dst_ref=cosin.at[step, part],
            send_sem=row_send.at[0], recv_sem=row_recv.at[STEPS + step],
            device_id={"row": peer}, device_id_type=MESH,
        )

    def message(part, peer):
        return to_blk(mgath.at[part], mgath.at[part], send.at[MEASURE], recv.at[MEASURE], peer)

    def tell_in(semaphore, peer):
        pl.semaphore_signal(semaphore, inc=1, device_id={"blk": peer}, device_id_type=MESH)

    def round_start(k):
        tell_in(up.at[k], lax.rem(blk + 2**k, blk_count))
        tell_in(down.at[k], lax.rem(blk + blk_count - 2**k, blk_count))

    def round_end(k):
        pl.semaphore_wait(up.at[k], 1)
        pl.semaphore_wait(down.at[k], 1)

    def first_loads():
        for i in range(-(-early * loads // chunks)):
            load(i).wait()

    @pl.when(even)
    def _():
        pl.semaphore_wait(barrier, 1)
        tell_in(hello.at[0], after)
        first_loads()
        for i in range(early):
            raw_next(span(i, i + 1)).start()

    @pl.when(odd)
    def _():
        first_loads()
        pl.semaphore_wait(hello.at[0], 1)
        for i in range(early):
            raw_below(span(i, i + 1), i).start()
        pl.semaphore_wait(barrier, row_count)
        tell_in(hello.at[0], after)
        tell_row(hello.at[1])

    def add_gram(left, right):
        lh, ll = split(left)
        rh, rl = split(right)
        acc[...] += lax.dot_general(
            jnp.concatenate([lh, ll], axis=1),
            jnp.concatenate([rh, rl], axis=1),
            (((0,), (0,)), ((), ())),
            preferred_element_type=F32,
        )
        norms[0:8] += jnp.sum((left * left).reshape(-1, 8, width), axis=0)
        norms[8:16] += jnp.sum((right * right).reshape(-1, 8, width), axis=0)

    def clear():
        acc[...] = jnp.zeros_like(acc)
        norms[...] = jnp.zeros_like(norms)

    def mix(slot, cosines):
        top, bottom = mixing(cosines)
        high, low = split(top)
        weights[slot, 0, :width] = high
        weights[slot, 1, :width] = low
        high, low = split(bottom)
        weights[slot, 0, width:] = high
        weights[slot, 1, width:] = low

    lane = lax.broadcasted_iota(jnp.int32, (1, width), 1)

    def row_peer(k):
        return lax.rem(row + k, row_count)

    def exchange(step):
        def copy(owners, peer):
            return pltpu.make_async_remote_copy(
                src_ref=gath.at[step, owners], dst_ref=gath.at[step, owners],
                send_sem=row_send.at[0], recv_sem=row_recv.at[step],
                device_id={"row": peer}, device_id_type=MESH,
            )

        gath[step, row, 0:width] = (
            acc[:width, :width] + acc[:width, width:] + acc[width:, :width]
        ) + acc[width:, width:]
        first = jnp.sum(norms[0:8], axis=0, keepdims=True)
        second = jnp.sum(norms[8:16], axis=0, keepdims=True)
        gath[step, row, width:width + 8] = jnp.broadcast_to(first, (8, width))
        gath[step, row, width + 8:width + 16] = jnp.broadcast_to(second, (8, width))
        for k in range(1, row_count):
            copy(pl.ds(row, 1), row_peer(k)).start()
        all_copies = copy(pl.ds(0, row_count - 1), row_peer(1))
        all_copies.wait_recv()
        total = gath[step, 0]
        for r in range(1, row_count):
            total = total + gath[step, r]
        all_copies.wait_send()
        cross = total[:width]
        first = lax.rsqrt(jnp.broadcast_to(total[width:width + 1], (width, width))).T
        second = lax.rsqrt(jnp.broadcast_to(total[width + 8:width + 9], (width, width)))
        cosines = cross * first * second
        coses[step] = cosines
        cos_move(step).start()
        mix(0, cosines)
        summed = jnp.sum(cosines * cosines, keepdims=True)
        own = jnp.where(lane == step, jnp.broadcast_to(summed, (1, width)), 0.0)
        if step == 0:
            mgath[blk] = own
        else:
            mgath[blk] += own

    def mix_below(step):
        cos_move(step).wait_recv()
        for k in range(1, row_count):
            cos_copy(step, at(row, share), row_peer(k)).start()
        all_copies = cos_copy(step, pl.ds(0, (row_count - 1) * share), row_peer(1))
        all_copies.wait_recv()
        mix(1, cosin[step])
        all_copies.wait_send()

    def transform(slot, left, right):
        lh, ll = split(left)
        rh, rl = split(right)
        high = jnp.concatenate([lh, rh], axis=1)
        low = jnp.concatenate([ll, rl], axis=1)
        own, fine = weights[slot, 0], weights[slot, 1]
        return dot(high, own) + (dot(high, fine) + dot(low, own))

    clear()

    def gram0(i, carry):
        @pl.when(i * chunks >= early * loads)
        def _():
            load(i).wait()

        part = at(i, gram_chunk)
        add_gram(xv[part, 0:width], xv[part, width:both])
        return carry

    lax.fori_loop(0, rows // gram_chunk, gram0, 0)

    @pl.when(odd)
    def _():
        pl.semaphore_wait(hello.at[1], row_count - 1)
        tell_in(hello.at[1], below)

    @pl.when(even)
    def _():
        pl.semaphore_wait(hello.at[0], 1)
        pl.semaphore_wait(hello.at[1], 1)

    round_start(0)
    exchange(0)
    round_end(0)

    def turn0(i, carry):
        part = at(i, chunk)
        mixed = transform(0, xv[part, 0:width], xv[part, width:both])
        move0[part] = mixed[:, :width]
        stay0[part] = mixed[:, width:]

        @pl.when(jnp.logical_and(i == 3, inner))
        def _():
            skip_move(span(0, ahead)).start()

        @pl.when(jnp.logical_and(i == 3, last))
        def _():
            skip_move(span(0, ahead_last)).start()

        @pl.when(jnp.logical_and(i > early, jnp.logical_not(inner)))
        def _():
            first_move(at(i - 1, chunk), i - 1).start()

        return carry

    lax.fori_loop(0, chunks, turn0, 0)

    if widen > 1:
        round_start(1)

    def start_first(i, carry):
        first_move(at(i, chunk), i).start()
        return carry

    def start_hold(i, carry):
        hold_move(at(i, chunk), i).start()
        return carry

    @pl.when(odd)
    def _():
        lax.fori_loop(early, passing, start_hold, 0)

    def start_hold_end(amount):
        if amount > int(amount):
            hold_move(span(int(amount), amount), int(amount)).start()

    for_each(after, start_hold_end, odd)

    @pl.when(inner)
    def _():
        raw_below(span(0, early), 0).wait_send()
        tell_row(hello.at[2])
        pl.semaphore_wait(hello.at[2], row_count - 1)
        skip_move(span(ahead, before_first)).start()
        lax.fori_loop(early, chunks, start_first, 0)

    def skip_between(amount):
        skip_move(span(before_first, after_first - given[3] + amount)).start()

    for_each(after, skip_between, inner, (2, 3))

    @pl.when(last)
    def _():
        start_first(chunks - 1, 0)
        skip_move(span(ahead_last, given[1])).start()

    @pl.when(even)
    def _():
        start_first(chunks - 1, 0)

    def give(amount):
        give_move(span(early, amount)).start()

    for_each(after, give, even)

    @pl.when(even)
    def _():
        for i in range(early):
            part = span(i, i + 1)
            raw_below(part, i).wait_recv()
            raw_on(part).start()

    def skip_all(amount):
        skip_move(span(0, amount)).start()

    for_each(second, skip_all, even)

    mix_below(0)
    raw_next(span(0, early)).wait_recv()
    clear()

    def early0(i, carry):
        part = at(i, chunk)
        mixed = transform(1, raw[part, 0:width], raw[part, width:both])
        come0[part] = mixed[:, :width]
        rest[part] = mixed[:, width:]
        add_gram(mixed[:, :width], stay0[part])
        return carry

    lax.fori_loop(0, early, early0, 0)

    def gram1(i, carry):
        part = at(i, chunk)
        first_move(part, i).wait_recv()

        add_gram(come0[part], stay0[part])
        return carry

    lax.fori_loop(early, chunks, gram1, 0)
    def pass_rest(start, stop):
        def pass_on(i, carry):
            part = at(i, chunk)
            hold_move(part, i).wait_recv()
            pass_move(part).start()
            return carry

        @pl.when(even)
        def _():
            lax.fori_loop(early + start, stop, pass_on, 0)

    def pass_end(amount):
        if amount > int(amount):
            part = span(int(amount), amount)
            hold_move(part, int(amount)).wait_recv()
            pass_move(part).start()

    pass_rest(0, early + 1)
    exchange(1)
    pass_rest(1, early + 2)
    for k in range(1, widen):
        if k > 1:
            round_start(k)
        round_end(k)

    def tell(k, carry):
        message(pl.ds(blk, 1), lax.rem(blk + k, blk_count)).start()
        return carry

    lax.fori_loop(1, blk_count, tell, 0)

    def hold_sent(amount):
        hold_move(span(early, amount), early).wait_send()

    def turn1(i, carry):
        part = at(i, chunk)
        mixed = transform(0, come0[part], stay0[part])
        out_ref[part, 0:width] = mixed[:, :width]
        move1[part] = mixed[:, width:]

        @pl.when(jnp.logical_and(i == passing + 1, inner))
        def _():
            for_each(after, hold_sent)

        def skip_end(amount):
            skip_move(span(after_first - given[3] + amount, given[4])).start()

        for_each(after, skip_end, jnp.logical_and(i == passing + 1, inner), (2, 3))

        def begin_second(amount):
            second_move(span(amount, int(amount) + 1)).start()

        for_each(after, begin_second, i == passing + 1)

        @pl.when(i > passing + 1)
        def _():
            second_move(at(i - 1, chunk)).start()

        return carry

    lax.fori_loop(passing, chunks, turn1, 0)
    second_move(span(chunks - 1, chunks)).start()

    pass_rest(2, whole_chunks(second))
    for_each(second, pass_end, even)

    def own1(i, carry):
        part = at(i, chunk)
        out_ref[part, 0:width] = transform(0, come0[part], stay0[part])[:, :width]
        return carry

    lax.fori_loop(0, passing, own1, 0)
    mix_below(1)

    def skip_rest_wait(amount):
        skip_move(span(0, amount)).wait_recv()
        give_move(span(early, amount)).wait_recv()

    for_each(blk, skip_rest_wait)

    def finish_part(part):
        out_ref[part, width:both] = transform(1, skip[part], rest[part])[:, width:]

    def early1(i, carry):
        finish_part(at(i, chunk))
        return carry

    lax.fori_loop(0, own_given, early1, 0)

    def early1_end(amount):
        if amount > int(amount):
            finish_part(span(int(amount), amount))

    for_each(blk, early1_end)
    messages = message(pl.ds(0, blk_count - 1), after)
    messages.wait_recv()
    off_ref[...] = jnp.sum(mgath[...], axis=0) / float(blk_count)

    messages.wait_send()
    first_move(span(early, chunks), early).wait_send()
    for step in range(STEPS):
        cos_move(step).wait_send()

    @pl.when(jnp.logical_not(inner))
    def _():
        raw_next(span(0, early)).wait_send()

    def skip_sent(amount):
        skip_move(span(0, amount)).wait_send()

    for_each(second, skip_sent)

    for_each(after, hold_sent, last)

    @pl.when(even)
    def _():
        raw_on(span(0, early)).wait_send()

    def give_sent(amount):
        give_move(span(early, amount)).wait_send()

    for_each(after, give_sent, even)

    def pass_sent(amount):
        pass_move(span(early, amount)).wait_send()

    for_each(second, pass_sent, even)

    def second_sent(amount):
        second_move(span(amount, chunks)).wait_send()

    for_each(after, second_sent)

    def second_arrived(amount):
        second_move(span(amount, chunks)).wait_recv()

    for_each(blk, second_arrived)


def settle(rotated, off, out_ref, off_ref, scalars, sem):
    whole = pltpu.make_async_copy(rotated, out_ref, sem.at[0])
    whole.start()
    values = off[...]
    lane = lax.broadcasted_iota(jnp.int32, values.shape, 1)
    for step in range(STEPS):
        scalars[step] = jnp.sum(jnp.where(lane == step, values, 0.0))
    few = pltpu.make_async_copy(scalars, off_ref, sem.at[1])
    few.start()
    few.wait()
    whole.wait()


def on_device(row_count, blk_count, matrix):
    rows, both = matrix.shape
    width = both // 2
    chunks, loads, early, given, _, _ = plan = 16, 4, 3, (9, 7.375, 8.5, 9, 7.75), (3, 3.25, 7.25), 2.5
    chunk = rows // chunks
    most = math.ceil(max(given))
    widen = 1
    while 2**widen < blk_count // 2:
        widen += 1
    dma = pltpu.SemaphoreType.DMA
    regular = pltpu.SemaphoreType.REGULAR
    block = pltpu.VMEM((rows, width), F32)
    some = pltpu.VMEM((most * chunk, width), F32)
    few = pltpu.VMEM((early * chunk, both), F32)
    vmem = pl.BlockSpec(memory_space=pltpu.VMEM)
    hbm = pl.BlockSpec(memory_space=pltpu.HBM)
    rotated, off = pl.pallas_call(
        functools.partial(kernel, row_count, blk_count, plan),
        out_shape=(
            jax.ShapeDtypeStruct((rows, both), F32),
            jax.ShapeDtypeStruct((1, width), F32),
        ),
        in_specs=[hbm],
        out_specs=(vmem, vmem),
        scratch_shapes=[
            pltpu.VMEM((rows, both), F32),
            block, block, block, some, block,
            few, few, some, some,
            pltpu.VMEM((both, both), F32),
            pltpu.VMEM((16, width), F32),
            pltpu.VMEM((STEPS, row_count, width + 16, width), F32),
            pltpu.VMEM((2, 2, both, both), BF16),
            pltpu.VMEM((STEPS, width, width), F32),
            pltpu.VMEM((STEPS, width, width), F32),
            pltpu.VMEM((blk_count, 1, width), F32),
            dma((loads,)), dma((early,)), dma((most - early,)), dma((chunks - early,)),
            dma((1,)), dma((2 * STEPS,)), dma((8 + STEPS,)), dma((5 + STEPS,)),
            regular((3,)), regular((widen,)), regular((widen,)),
        ],
        compiler_params=pltpu.CompilerParams(
            collective_id=0, has_side_effects=True, vmem_limit_bytes=48 * 1024 * 1024
        ),
    )(matrix)
    return pl.pallas_call(
        settle,
        out_shape=(
            jax.ShapeDtypeStruct((rows, both), F32),
            jax.ShapeDtypeStruct((STEPS,), F32),
        ),
        in_specs=[vmem, vmem],
        out_specs=(hbm, hbm),
        scratch_shapes=[pltpu.SMEM((STEPS,), F32), dma((2,))],
        compiler_params=pltpu.CompilerParams(vmem_limit_bytes=8 * 1024 * 1024),
    )(rotated, off)


def solution(mesh):
    return jax.shard_map(
        functools.partial(on_device, mesh.shape["row"], mesh.shape["blk"]),
        mesh=mesh,
        in_specs=(P("row", "blk"),),
        out_specs=(P("row", "blk"), P()),
        check_vma=False,
    )
```

```python
import functools
import math

import jax
import jax.numpy as jnp
from jax import lax
from jax.experimental import pallas as pl
from jax.experimental.pallas import tpu as pltpu
from jax.sharding import PartitionSpec as P

STEPS = 2
NS_ITERS = 4
MESH = pl.DeviceIdType.MESH
F32 = jnp.float32
BF16 = jnp.bfloat16


def split(value):
    high = value.astype(BF16)
    return high, (value - high.astype(F32)).astype(BF16)


def dot(a, b):
    return jnp.dot(a, b, preferred_element_type=F32)


def product(a, b):
    ah, al = split(a)
    bh, bl = split(b)
    width = b.shape[1]
    both = dot(
        jnp.concatenate([ah, al], axis=1),
        jnp.concatenate(
            [
                jnp.concatenate([bh, bl], axis=1),
                jnp.concatenate([bh, jnp.zeros_like(bl)], axis=1),
            ],
            axis=0,
        ),
    )
    return both[:, :width] + both[:, width:]


def mixing(cosines):
    width = cosines.shape[0]
    rows = lax.broadcasted_iota(jnp.int32, (width, width), 0)
    columns = lax.broadcasted_iota(jnp.int32, (width, width), 1)
    identity = jnp.where(rows == columns, 1.0, 0.0).astype(F32)
    coupling = 0.5 * cosines
    flipped = coupling.T
    scale = 1.0 + jnp.sum(coupling * coupling, keepdims=True)
    shrink = 1.0 / scale
    current = [
        (identity + product(coupling, flipped)) * shrink,
        (identity + product(flipped, coupling)) * shrink,
    ]
    result = [None, None]
    for count in range(NS_ITERS):
        for side in range(2):
            y, z = current[side], result[side]
            inner = y if z is None else product(z, y)
            factor = 1.5 * identity - 0.5 * inner
            if count < NS_ITERS - 1:
                current[side] = product(y, factor)
            result[side] = factor if z is None else product(factor, z)
    root = 1.0 / jnp.sqrt(scale)
    first, second = result[0] * root, result[1] * root
    return (
        jnp.concatenate([first, product(coupling, second)], axis=1),
        jnp.concatenate([-product(flipped, first), second], axis=1),
    )


def kernel(
    row_count, blk_count, plan, x_hbm, out_ref, off_ref,
    xv, move0, stay0, come0, rest, move1, raw, via, skip, hold,
    acc, norms, gath, weights, coses, cosin, mgath,
    load_sem, via_recv, hold_recv, first_recv, row_send, row_recv, send, recv, hello, up, down,
):
    rows, both = x_hbm.shape
    width = both // 2
    chunks, loads, early, given, pieces, ahead_last = plan
    ahead, before_first, after_first = pieces
    chunk, gram_chunk = rows // chunks, rows // loads
    widen = up.shape[0]
    share = width // row_count
    row, blk = lax.axis_index("row"), lax.axis_index("blk")
    after = lax.rem(blk + 1, blk_count)
    second = lax.rem(blk + 2, blk_count)
    below = lax.rem(blk + blk_count - 1, blk_count)
    odd = lax.rem(blk, 2) == 1
    even = jnp.logical_not(odd)
    last = blk == blk_count - 1
    inner = jnp.logical_and(odd, jnp.logical_not(last))

    def each(target):
        others, parity = target > 2, lax.rem(target, 2)
        return [
            (given[0], target == 0),
            (given[1], target == 1),
            (given[2], target == 2),
            (given[3], jnp.logical_and(others, parity == 0)),
            (given[4], jnp.logical_and(others, parity == 1)),
        ]

    def whole_chunks(target):
        count = jnp.int32(0)
        for amount, chosen in each(target):
            count = jnp.where(chosen, jnp.int32(int(amount)), count)
        return count

    def for_each(target, act, also=None, kinds=range(5)):
        for kind in kinds:
            amount, chosen = each(target)[kind]
            pl.when(chosen if also is None else jnp.logical_and(chosen, also))(
                functools.partial(act, amount)
            )

    passing, own_given = whole_chunks(after), whole_chunks(blk)

    barrier = pltpu.get_barrier_semaphore()
    pl.semaphore_signal(barrier, inc=1, device_id={"blk": below}, device_id_type=MESH)

    def tell_row(semaphore):
        for k in range(1, row_count):
            pl.semaphore_signal(
                semaphore, inc=1, device_id={"row": lax.rem(row + k, row_count)},
                device_id_type=MESH,
            )

    @pl.when(odd)
    def _():
        tell_row(barrier)

    def at(i, size):
        return pl.ds(pl.multiple_of(i * size, size), size)

    def span(first, last):
        return pl.ds(int(first * chunk), int((last - first) * chunk))

    def load(i):
        return pltpu.make_async_copy(
            x_hbm.at[at(i, gram_chunk)], xv.at[at(i, gram_chunk)], load_sem.at[i]
        )

    def start_load(i, carry):
        load(i).start()
        return carry

    lax.fori_loop(0, rows // gram_chunk, start_load, 0)

    def to_blk(source, target, send, recv, peer):
        return pltpu.make_async_remote_copy(
            src_ref=source, dst_ref=target, send_sem=send, recv_sem=recv,
            device_id={"blk": peer}, device_id_type=MESH,
        )

    RAW, SKIP, REST, SECOND, MEASURE, COS, FIRST, ON = 0, 1, 2, 3, 4, 5, 5 + STEPS, 6 + STEPS
    right = pl.ds(width, width)

    def raw_next(part):
        return to_blk(xv.at[part], raw.at[part], send.at[RAW], recv.at[RAW], after)

    def raw_below(part, i):
        return to_blk(xv.at[part], via.at[part], send.at[RAW], via_recv.at[i], below)

    def raw_on(part):
        return to_blk(via.at[part], raw.at[part], send.at[ON], recv.at[RAW], second)

    def skip_move(part):
        return to_blk(move0.at[part], skip.at[part], send.at[SKIP], recv.at[SKIP], second)

    def first_move(part, i):
        return to_blk(
            move0.at[part], come0.at[part], send.at[FIRST], first_recv.at[i - early], after
        )

    def second_move(part):
        return to_blk(
            move1.at[part], out_ref.at[part, right], send.at[SECOND], recv.at[SECOND], after
        )

    def give_move(part):
        return to_blk(stay0.at[part], rest.at[part], send.at[REST], recv.at[REST], after)

    def hold_move(part, i):
        return to_blk(stay0.at[part], hold.at[part], send.at[REST], hold_recv.at[i - early], below)

    def pass_move(part):
        return to_blk(hold.at[part], rest.at[part], send.at[ON + 1], recv.at[REST], second)

    def cos_move(step):
        part = at(row, share)
        return to_blk(
            coses.at[step, part], cosin.at[step, part], send.at[COS + step], recv.at[COS + step],
            after,
        )

    def cos_copy(step, part, peer):
        return pltpu.make_async_remote_copy(
            src_ref=cosin.at[step, part], dst_ref=cosin.at[step, part],
            send_sem=row_send.at[0], recv_sem=row_recv.at[STEPS + step],
            device_id={"row": peer}, device_id_type=MESH,
        )

    def message(part, peer):
        return to_blk(mgath.at[part], mgath.at[part], send.at[MEASURE], recv.at[MEASURE], peer)

    def tell_in(semaphore, peer):
        pl.semaphore_signal(semaphore, inc=1, device_id={"blk": peer}, device_id_type=MESH)

    def round_start(k):
        tell_in(up.at[k], lax.rem(blk + 2**k, blk_count))
        tell_in(down.at[k], lax.rem(blk + blk_count - 2**k, blk_count))

    def round_end(k):
        pl.semaphore_wait(up.at[k], 1)
        pl.semaphore_wait(down.at[k], 1)

    def first_loads():
        for i in range(-(-early * loads // chunks)):
            load(i).wait()

    @pl.when(even)
    def _():
        pl.semaphore_wait(barrier, 1)
        tell_in(hello.at[0], after)
        first_loads()
        for i in range(early):
            raw_next(span(i, i + 1)).start()

    @pl.when(odd)
    def _():
        first_loads()
        pl.semaphore_wait(hello.at[0], 1)
        for i in range(early):
            raw_below(span(i, i + 1), i).start()
        pl.semaphore_wait(barrier, row_count)
        tell_in(hello.at[0], after)
        tell_row(hello.at[1])

    def add_gram(left, right):
        lh, ll = split(left)
        rh, rl = split(right)
        acc[...] += lax.dot_general(
            jnp.concatenate([lh, ll], axis=1),
            jnp.concatenate([rh, rl], axis=1),
            (((0,), (0,)), ((), ())),
            preferred_element_type=F32,
        )
        norms[0:8] += jnp.sum((left * left).reshape(-1, 8, width), axis=0)
        norms[8:16] += jnp.sum((right * right).reshape(-1, 8, width), axis=0)

    def clear():
        acc[...] = jnp.zeros_like(acc)
        norms[...] = jnp.zeros_like(norms)

    def mix(slot, cosines):
        top, bottom = mixing(cosines)
        high, low = split(top)
        weights[slot, 0, :width] = high
        weights[slot, 1, :width] = low
        high, low = split(bottom)
        weights[slot, 0, width:] = high
        weights[slot, 1, width:] = low

    lane = lax.broadcasted_iota(jnp.int32, (1, width), 1)

    def row_peer(k):
        return lax.rem(row + k, row_count)

    def exchange(step):
        def copy(owners, peer):
            return pltpu.make_async_remote_copy(
                src_ref=gath.at[step, owners], dst_ref=gath.at[step, owners],
                send_sem=row_send.at[0], recv_sem=row_recv.at[step],
                device_id={"row": peer}, device_id_type=MESH,
            )

        gath[step, row, 0:width] = (
            acc[:width, :width] + acc[:width, width:] + acc[width:, :width]
        ) + acc[width:, width:]
        first = jnp.sum(norms[0:8], axis=0, keepdims=True)
        second = jnp.sum(norms[8:16], axis=0, keepdims=True)
        gath[step, row, width:width + 8] = jnp.broadcast_to(first, (8, width))
        gath[step, row, width + 8:width + 16] = jnp.broadcast_to(second, (8, width))
        for k in range(1, row_count):
            copy(pl.ds(row, 1), row_peer(k)).start()
        all_copies = copy(pl.ds(0, row_count - 1), row_peer(1))
        all_copies.wait_recv()
        total = gath[step, 0]
        for r in range(1, row_count):
            total = total + gath[step, r]
        all_copies.wait_send()
        cross = total[:width]
        first = lax.rsqrt(jnp.broadcast_to(total[width:width + 1], (width, width))).T
        second = lax.rsqrt(jnp.broadcast_to(total[width + 8:width + 9], (width, width)))
        cosines = cross * first * second
        coses[step] = cosines
        cos_move(step).start()
        mix(0, cosines)
        summed = jnp.sum(cosines * cosines, keepdims=True)
        own = jnp.where(lane == step, jnp.broadcast_to(summed, (1, width)), 0.0)
        if step == 0:
            mgath[blk] = own
        else:
            mgath[blk] += own

    def mix_below(step):
        cos_move(step).wait_recv()
        for k in range(1, row_count):
            cos_copy(step, at(row, share), row_peer(k)).start()
        all_copies = cos_copy(step, pl.ds(0, (row_count - 1) * share), row_peer(1))
        all_copies.wait_recv()
        mix(1, cosin[step])
        all_copies.wait_send()

    def transform(slot, left, right):
        lh, ll = split(left)
        rh, rl = split(right)
        high = jnp.concatenate([lh, rh], axis=1)
        low = jnp.concatenate([ll, rl], axis=1)
        own, fine = weights[slot, 0], weights[slot, 1]
        return dot(high, own) + (dot(high, fine) + dot(low, own))

    clear()

    def gram0(i, carry):
        @pl.when(i * chunks >= early * loads)
        def _():
            load(i).wait()

        part = at(i, gram_chunk)
        add_gram(xv[part, 0:width], xv[part, width:both])
        return carry

    lax.fori_loop(0, rows // gram_chunk, gram0, 0)

    @pl.when(odd)
    def _():
        pl.semaphore_wait(hello.at[1], row_count - 1)
        tell_in(hello.at[1], below)

    @pl.when(even)
    def _():
        pl.semaphore_wait(hello.at[0], 1)
        pl.semaphore_wait(hello.at[1], 1)

    round_start(0)
    exchange(0)
    round_end(0)

    def turn0(i, carry):
        part = at(i, chunk)
        mixed = transform(0, xv[part, 0:width], xv[part, width:both])
        move0[part] = mixed[:, :width]
        stay0[part] = mixed[:, width:]

        @pl.when(jnp.logical_and(i == 3, inner))
        def _():
            skip_move(span(0, ahead)).start()

        @pl.when(jnp.logical_and(i == 3, last))
        def _():
            skip_move(span(0, ahead_last)).start()

        @pl.when(jnp.logical_and(i > early, jnp.logical_not(inner)))
        def _():
            first_move(at(i - 1, chunk), i - 1).start()

        return carry

    lax.fori_loop(0, chunks, turn0, 0)

    if widen > 1:
        round_start(1)

    def start_first(i, carry):
        first_move(at(i, chunk), i).start()
        return carry

    def start_hold(i, carry):
        hold_move(at(i, chunk), i).start()
        return carry

    @pl.when(odd)
    def _():
        lax.fori_loop(early, passing, start_hold, 0)

    def start_hold_end(amount):
        if amount > int(amount):
            hold_move(span(int(amount), amount), int(amount)).start()

    for_each(after, start_hold_end, odd)

    @pl.when(inner)
    def _():
        raw_below(span(0, early), 0).wait_send()
        tell_row(hello.at[2])
        pl.semaphore_wait(hello.at[2], row_count - 1)
        skip_move(span(ahead, before_first)).start()
        lax.fori_loop(early, chunks, start_first, 0)

    def skip_between(amount):
        skip_move(span(before_first, after_first - given[3] + amount)).start()

    for_each(after, skip_between, inner, (2, 3))

    @pl.when(last)
    def _():
        start_first(chunks - 1, 0)
        skip_move(span(ahead_last, given[1])).start()

    @pl.when(even)
    def _():
        start_first(chunks - 1, 0)

    def give(amount):
        give_move(span(early, amount)).start()

    for_each(after, give, even)

    @pl.when(even)
    def _():
        for i in range(early):
            part = span(i, i + 1)
            raw_below(part, i).wait_recv()
            raw_on(part).start()

    def skip_all(amount):
        skip_move(span(0, amount)).start()

    for_each(second, skip_all, even)

    mix_below(0)
    raw_next(span(0, early)).wait_recv()
    clear()

    def early0(i, carry):
        part = at(i, chunk)
        mixed = transform(1, raw[part, 0:width], raw[part, width:both])
        come0[part] = mixed[:, :width]
        rest[part] = mixed[:, width:]
        add_gram(mixed[:, :width], stay0[part])
        return carry

    lax.fori_loop(0, early, early0, 0)

    def gram1(i, carry):
        part = at(i, chunk)
        first_move(part, i).wait_recv()

        add_gram(come0[part], stay0[part])
        return carry

    lax.fori_loop(early, chunks, gram1, 0)
    def pass_rest(start, stop):
        def pass_on(i, carry):
            part = at(i, chunk)
            hold_move(part, i).wait_recv()
            pass_move(part).start()
            return carry

        @pl.when(even)
        def _():
            lax.fori_loop(early + start, stop, pass_on, 0)

    def pass_end(amount):
        if amount > int(amount):
            part = span(int(amount), amount)
            hold_move(part, int(amount)).wait_recv()
            pass_move(part).start()

    pass_rest(0, early + 1)
    exchange(1)
    pass_rest(1, early + 2)
    for k in range(1, widen):
        if k > 1:
            round_start(k)
        round_end(k)

    def tell(k, carry):
        message(pl.ds(blk, 1), lax.rem(blk + k, blk_count)).start()
        return carry

    lax.fori_loop(1, blk_count, tell, 0)

    def hold_sent(amount):
        hold_move(span(early, amount), early).wait_send()

    def turn1(i, carry):
        part = at(i, chunk)
        mixed = transform(0, come0[part], stay0[part])
        out_ref[part, 0:width] = mixed[:, :width]
        move1[part] = mixed[:, width:]

        @pl.when(jnp.logical_and(i == passing + 1, inner))
        def _():
            for_each(after, hold_sent)

        def skip_end(amount):
            skip_move(span(after_first - given[3] + amount, given[4])).start()

        for_each(after, skip_end, jnp.logical_and(i == passing + 1, inner), (2, 3))

        def begin_second(amount):
            second_move(span(amount, int(amount) + 1)).start()

        for_each(after, begin_second, i == passing + 1)

        @pl.when(i > passing + 1)
        def _():
            second_move(at(i - 1, chunk)).start()

        return carry

    lax.fori_loop(passing, chunks, turn1, 0)
    second_move(span(chunks - 1, chunks)).start()

    pass_rest(2, whole_chunks(second))
    for_each(second, pass_end, even)

    def own1(i, carry):
        part = at(i, chunk)
        out_ref[part, 0:width] = transform(0, come0[part], stay0[part])[:, :width]
        return carry

    lax.fori_loop(0, passing, own1, 0)
    mix_below(1)

    def skip_rest_wait(amount):
        skip_move(span(0, amount)).wait_recv()
        give_move(span(early, amount)).wait_recv()

    for_each(blk, skip_rest_wait)

    def finish_part(part):
        out_ref[part, width:both] = transform(1, skip[part], rest[part])[:, width:]

    def early1(i, carry):
        finish_part(at(i, chunk))
        return carry

    lax.fori_loop(0, own_given, early1, 0)

    def early1_end(amount):
        if amount > int(amount):
            finish_part(span(int(amount), amount))

    for_each(blk, early1_end)
    messages = message(pl.ds(0, blk_count - 1), after)
    messages.wait_recv()
    off_ref[...] = jnp.sum(mgath[...], axis=0) / float(blk_count)

    messages.wait_send()
    first_move(span(early, chunks), early).wait_send()
    for step in range(STEPS):
        cos_move(step).wait_send()

    @pl.when(jnp.logical_not(inner))
    def _():
        raw_next(span(0, early)).wait_send()

    def skip_sent(amount):
        skip_move(span(0, amount)).wait_send()

    for_each(second, skip_sent)

    for_each(after, hold_sent, last)

    @pl.when(even)
    def _():
        raw_on(span(0, early)).wait_send()

    def give_sent(amount):
        give_move(span(early, amount)).wait_send()

    for_each(after, give_sent, even)

    def pass_sent(amount):
        pass_move(span(early, amount)).wait_send()

    for_each(second, pass_sent, even)

    def second_sent(amount):
        second_move(span(amount, chunks)).wait_send()

    for_each(after, second_sent)

    def second_arrived(amount):
        second_move(span(amount, chunks)).wait_recv()

    for_each(blk, second_arrived)


def settle(rotated, off, out_ref, off_ref, scalars, sem):
    whole = pltpu.make_async_copy(rotated, out_ref, sem.at[0])
    whole.start()
    values = off[...]
    lane = lax.broadcasted_iota(jnp.int32, values.shape, 1)
    for step in range(STEPS):
        scalars[step] = jnp.sum(jnp.where(lane == step, values, 0.0))
    few = pltpu.make_async_copy(scalars, off_ref, sem.at[1])
    few.start()
    few.wait()
    whole.wait()


def on_device(row_count, blk_count, matrix):
    rows, both = matrix.shape
    width = both // 2
    chunks, loads, early, given, _, _ = plan = 16, 4, 3, (9, 7.25, 8.5, 9, 7.75), (3, 3.25, 7.25), 2.5
    chunk = rows // chunks
    most = math.ceil(max(given))
    widen = 1
    while 2**widen < blk_count // 2:
        widen += 1
    dma = pltpu.SemaphoreType.DMA
    regular = pltpu.SemaphoreType.REGULAR
    block = pltpu.VMEM((rows, width), F32)
    some = pltpu.VMEM((most * chunk, width), F32)
    few = pltpu.VMEM((early * chunk, both), F32)
    vmem = pl.BlockSpec(memory_space=pltpu.VMEM)
    hbm = pl.BlockSpec(memory_space=pltpu.HBM)
    rotated, off = pl.pallas_call(
        functools.partial(kernel, row_count, blk_count, plan),
        out_shape=(
            jax.ShapeDtypeStruct((rows, both), F32),
            jax.ShapeDtypeStruct((1, width), F32),
        ),
        in_specs=[hbm],
        out_specs=(vmem, vmem),
        scratch_shapes=[
            pltpu.VMEM((rows, both), F32),
            block, block, block, some, block,
            few, few, some, some,
            pltpu.VMEM((both, both), F32),
            pltpu.VMEM((16, width), F32),
            pltpu.VMEM((STEPS, row_count, width + 16, width), F32),
            pltpu.VMEM((2, 2, both, both), BF16),
            pltpu.VMEM((STEPS, width, width), F32),
            pltpu.VMEM((STEPS, width, width), F32),
            pltpu.VMEM((blk_count, 1, width), F32),
            dma((loads,)), dma((early,)), dma((most - early,)), dma((chunks - early,)),
            dma((1,)), dma((2 * STEPS,)), dma((8 + STEPS,)), dma((5 + STEPS,)),
            regular((3,)), regular((widen,)), regular((widen,)),
        ],
        compiler_params=pltpu.CompilerParams(
            collective_id=0, has_side_effects=True, vmem_limit_bytes=48 * 1024 * 1024
        ),
    )(matrix)
    return pl.pallas_call(
        settle,
        out_shape=(
            jax.ShapeDtypeStruct((rows, both), F32),
            jax.ShapeDtypeStruct((STEPS,), F32),
        ),
        in_specs=[vmem, vmem],
        out_specs=(hbm, hbm),
        scratch_shapes=[pltpu.SMEM((STEPS,), F32), dma((2,))],
        compiler_params=pltpu.CompilerParams(vmem_limit_bytes=8 * 1024 * 1024),
    )(rotated, off)


def solution(mesh):
    return jax.shard_map(
        functools.partial(on_device, mesh.shape["row"], mesh.shape["blk"]),
        mesh=mesh,
        in_specs=(P("row", "blk"),),
        out_specs=(P("row", "blk"), P()),
        check_vma=False,
    )
```

```python
import functools
import math

import jax
import jax.numpy as jnp
from jax import lax
from jax.experimental import pallas as pl
from jax.experimental.pallas import tpu as pltpu
from jax.sharding import PartitionSpec as P

STEPS = 2
NS_ITERS = 4
MESH = pl.DeviceIdType.MESH
F32 = jnp.float32
BF16 = jnp.bfloat16


def split(value):
    high = value.astype(BF16)
    return high, (value - high.astype(F32)).astype(BF16)


def dot(a, b):
    return jnp.dot(a, b, preferred_element_type=F32)


def product(a, b):
    ah, al = split(a)
    bh, bl = split(b)
    width = b.shape[1]
    both = dot(
        jnp.concatenate([ah, al], axis=1),
        jnp.concatenate(
            [
                jnp.concatenate([bh, bl], axis=1),
                jnp.concatenate([bh, jnp.zeros_like(bl)], axis=1),
            ],
            axis=0,
        ),
    )
    return both[:, :width] + both[:, width:]


def mixing(cosines):
    width = cosines.shape[0]
    rows = lax.broadcasted_iota(jnp.int32, (width, width), 0)
    columns = lax.broadcasted_iota(jnp.int32, (width, width), 1)
    identity = jnp.where(rows == columns, 1.0, 0.0).astype(F32)
    coupling = 0.5 * cosines
    flipped = coupling.T
    scale = 1.0 + jnp.sum(coupling * coupling, keepdims=True)
    shrink = 1.0 / scale
    current = [
        (identity + product(coupling, flipped)) * shrink,
        (identity + product(flipped, coupling)) * shrink,
    ]
    result = [None, None]
    for count in range(NS_ITERS):
        for side in range(2):
            y, z = current[side], result[side]
            inner = y if z is None else product(z, y)
            factor = 1.5 * identity - 0.5 * inner
            if count < NS_ITERS - 1:
                current[side] = product(y, factor)
            result[side] = factor if z is None else product(factor, z)
    root = 1.0 / jnp.sqrt(scale)
    first, second = result[0] * root, result[1] * root
    return (
        jnp.concatenate([first, product(coupling, second)], axis=1),
        jnp.concatenate([-product(flipped, first), second], axis=1),
    )


def kernel(
    row_count, blk_count, plan, x_hbm, out_ref, off_ref,
    xv, move0, stay0, come0, rest, move1, raw, via, skip, hold,
    acc, norms, gath, weights, coses, cosin, mgath,
    load_sem, via_recv, hold_recv, first_recv, row_send, row_recv, send, recv, hello, up, down,
):
    rows, both = x_hbm.shape
    width = both // 2
    chunks, loads, early, given, pieces, ahead_last = plan
    ahead, before_first, after_first = pieces
    chunk, gram_chunk = rows // chunks, rows // loads
    widen = up.shape[0]
    share = width // row_count
    row, blk = lax.axis_index("row"), lax.axis_index("blk")
    after = lax.rem(blk + 1, blk_count)
    second = lax.rem(blk + 2, blk_count)
    below = lax.rem(blk + blk_count - 1, blk_count)
    odd = lax.rem(blk, 2) == 1
    even = jnp.logical_not(odd)
    last = blk == blk_count - 1
    inner = jnp.logical_and(odd, jnp.logical_not(last))

    def each(target):
        others, parity = target > 2, lax.rem(target, 2)
        return [
            (given[0], target == 0),
            (given[1], target == 1),
            (given[2], target == 2),
            (given[3], jnp.logical_and(others, parity == 0)),
            (given[4], jnp.logical_and(others, parity == 1)),
        ]

    def whole_chunks(target):
        count = jnp.int32(0)
        for amount, chosen in each(target):
            count = jnp.where(chosen, jnp.int32(int(amount)), count)
        return count

    def for_each(target, act, also=None, kinds=range(5)):
        for kind in kinds:
            amount, chosen = each(target)[kind]
            pl.when(chosen if also is None else jnp.logical_and(chosen, also))(
                functools.partial(act, amount)
            )

    passing, own_given = whole_chunks(after), whole_chunks(blk)

    barrier = pltpu.get_barrier_semaphore()
    pl.semaphore_signal(barrier, inc=1, device_id={"blk": below}, device_id_type=MESH)

    def tell_row(semaphore):
        for k in range(1, row_count):
            pl.semaphore_signal(
                semaphore, inc=1, device_id={"row": lax.rem(row + k, row_count)},
                device_id_type=MESH,
            )

    @pl.when(odd)
    def _():
        tell_row(barrier)

    def at(i, size):
        return pl.ds(pl.multiple_of(i * size, size), size)

    def span(first, last):
        return pl.ds(int(first * chunk), int((last - first) * chunk))

    def load(i):
        return pltpu.make_async_copy(
            x_hbm.at[at(i, gram_chunk)], xv.at[at(i, gram_chunk)], load_sem.at[i]
        )

    def start_load(i, carry):
        load(i).start()
        return carry

    lax.fori_loop(0, rows // gram_chunk, start_load, 0)

    def to_blk(source, target, send, recv, peer):
        return pltpu.make_async_remote_copy(
            src_ref=source, dst_ref=target, send_sem=send, recv_sem=recv,
            device_id={"blk": peer}, device_id_type=MESH,
        )

    RAW, SKIP, REST, SECOND, MEASURE, COS, FIRST, ON = 0, 1, 2, 3, 4, 5, 5 + STEPS, 6 + STEPS
    right = pl.ds(width, width)

    def raw_next(part):
        return to_blk(xv.at[part], raw.at[part], send.at[RAW], recv.at[RAW], after)

    def raw_below(part, i):
        return to_blk(xv.at[part], via.at[part], send.at[RAW], via_recv.at[i], below)

    def raw_on(part):
        return to_blk(via.at[part], raw.at[part], send.at[ON], recv.at[RAW], second)

    def skip_move(part):
        return to_blk(move0.at[part], skip.at[part], send.at[SKIP], recv.at[SKIP], second)

    def first_move(part, i):
        return to_blk(
            move0.at[part], come0.at[part], send.at[FIRST], first_recv.at[i - early], after
        )

    def second_move(part):
        return to_blk(
            move1.at[part], out_ref.at[part, right], send.at[SECOND], recv.at[SECOND], after
        )

    def give_move(part):
        return to_blk(stay0.at[part], rest.at[part], send.at[REST], recv.at[REST], after)

    def hold_move(part, i):
        return to_blk(stay0.at[part], hold.at[part], send.at[REST], hold_recv.at[i - early], below)

    def pass_move(part):
        return to_blk(hold.at[part], rest.at[part], send.at[ON + 1], recv.at[REST], second)

    def cos_move(step):
        part = at(row, share)
        return to_blk(
            coses.at[step, part], cosin.at[step, part], send.at[COS + step], recv.at[COS + step],
            after,
        )

    def cos_copy(step, part, peer):
        return pltpu.make_async_remote_copy(
            src_ref=cosin.at[step, part], dst_ref=cosin.at[step, part],
            send_sem=row_send.at[0], recv_sem=row_recv.at[STEPS + step],
            device_id={"row": peer}, device_id_type=MESH,
        )

    def message(part, peer):
        return to_blk(mgath.at[part], mgath.at[part], send.at[MEASURE], recv.at[MEASURE], peer)

    def tell_in(semaphore, peer):
        pl.semaphore_signal(semaphore, inc=1, device_id={"blk": peer}, device_id_type=MESH)

    def round_start(k):
        tell_in(up.at[k], lax.rem(blk + 2**k, blk_count))
        tell_in(down.at[k], lax.rem(blk + blk_count - 2**k, blk_count))

    def round_end(k):
        pl.semaphore_wait(up.at[k], 1)
        pl.semaphore_wait(down.at[k], 1)

    def first_loads():
        for i in range(-(-early * loads // chunks)):
            load(i).wait()

    @pl.when(even)
    def _():
        pl.semaphore_wait(barrier, 1)
        tell_in(hello.at[0], after)
        first_loads()
        for i in range(early):
            raw_next(span(i, i + 1)).start()

    @pl.when(odd)
    def _():
        first_loads()
        pl.semaphore_wait(hello.at[0], 1)
        for i in range(early):
            raw_below(span(i, i + 1), i).start()
        pl.semaphore_wait(barrier, row_count)
        tell_in(hello.at[0], after)
        tell_row(hello.at[1])

    def add_gram(left, right):
        lh, ll = split(left)
        rh, rl = split(right)
        acc[...] += lax.dot_general(
            jnp.concatenate([lh, ll], axis=1),
            jnp.concatenate([rh, rl], axis=1),
            (((0,), (0,)), ((), ())),
            preferred_element_type=F32,
        )
        norms[0:8] += jnp.sum((left * left).reshape(-1, 8, width), axis=0)
        norms[8:16] += jnp.sum((right * right).reshape(-1, 8, width), axis=0)

    def clear():
        acc[...] = jnp.zeros_like(acc)
        norms[...] = jnp.zeros_like(norms)

    def mix(slot, cosines):
        top, bottom = mixing(cosines)
        high, low = split(top)
        weights[slot, 0, :width] = high
        weights[slot, 1, :width] = low
        high, low = split(bottom)
        weights[slot, 0, width:] = high
        weights[slot, 1, width:] = low

    lane = lax.broadcasted_iota(jnp.int32, (1, width), 1)

    def row_peer(k):
        return lax.rem(row + k, row_count)

    def exchange(step):
        def copy(owners, peer):
            return pltpu.make_async_remote_copy(
                src_ref=gath.at[step, owners], dst_ref=gath.at[step, owners],
                send_sem=row_send.at[0], recv_sem=row_recv.at[step],
                device_id={"row": peer}, device_id_type=MESH,
            )

        gath[step, row, 0:width] = (
            acc[:width, :width] + acc[:width, width:] + acc[width:, :width]
        ) + acc[width:, width:]
        first = jnp.sum(norms[0:8], axis=0, keepdims=True)
        second = jnp.sum(norms[8:16], axis=0, keepdims=True)
        gath[step, row, width:width + 8] = jnp.broadcast_to(first, (8, width))
        gath[step, row, width + 8:width + 16] = jnp.broadcast_to(second, (8, width))
        for k in range(1, row_count):
            copy(pl.ds(row, 1), row_peer(k)).start()
        all_copies = copy(pl.ds(0, row_count - 1), row_peer(1))
        all_copies.wait_recv()
        total = gath[step, 0]
        for r in range(1, row_count):
            total = total + gath[step, r]
        all_copies.wait_send()
        cross = total[:width]
        first = lax.rsqrt(jnp.broadcast_to(total[width:width + 1], (width, width))).T
        second = lax.rsqrt(jnp.broadcast_to(total[width + 8:width + 9], (width, width)))
        cosines = cross * first * second
        coses[step] = cosines
        cos_move(step).start()
        mix(0, cosines)
        summed = jnp.sum(cosines * cosines, keepdims=True)
        own = jnp.where(lane == step, jnp.broadcast_to(summed, (1, width)), 0.0)
        if step == 0:
            mgath[blk] = own
        else:
            mgath[blk] += own

    def mix_below(step):
        cos_move(step).wait_recv()
        for k in range(1, row_count):
            cos_copy(step, at(row, share), row_peer(k)).start()
        all_copies = cos_copy(step, pl.ds(0, (row_count - 1) * share), row_peer(1))
        all_copies.wait_recv()
        mix(1, cosin[step])
        all_copies.wait_send()

    def transform(slot, left, right):
        lh, ll = split(left)
        rh, rl = split(right)
        high = jnp.concatenate([lh, rh], axis=1)
        low = jnp.concatenate([ll, rl], axis=1)
        own, fine = weights[slot, 0], weights[slot, 1]
        return dot(high, own) + (dot(high, fine) + dot(low, own))

    clear()

    def gram0(i, carry):
        @pl.when(i * chunks >= early * loads)
        def _():
            load(i).wait()

        part = at(i, gram_chunk)
        add_gram(xv[part, 0:width], xv[part, width:both])
        return carry

    lax.fori_loop(0, rows // gram_chunk, gram0, 0)

    @pl.when(odd)
    def _():
        pl.semaphore_wait(hello.at[1], row_count - 1)
        tell_in(hello.at[1], below)

    @pl.when(even)
    def _():
        pl.semaphore_wait(hello.at[0], 1)
        pl.semaphore_wait(hello.at[1], 1)

    round_start(0)
    exchange(0)
    round_end(0)

    def turn0(i, carry):
        part = at(i, chunk)
        mixed = transform(0, xv[part, 0:width], xv[part, width:both])
        move0[part] = mixed[:, :width]
        stay0[part] = mixed[:, width:]

        @pl.when(jnp.logical_and(i == 3, inner))
        def _():
            skip_move(span(0, ahead)).start()

        @pl.when(jnp.logical_and(i == 3, last))
        def _():
            skip_move(span(0, ahead_last)).start()

        @pl.when(jnp.logical_and(i > early, jnp.logical_not(inner)))
        def _():
            first_move(at(i - 1, chunk), i - 1).start()

        return carry

    lax.fori_loop(0, chunks, turn0, 0)

    if widen > 1:
        round_start(1)

    def start_first(i, carry):
        first_move(at(i, chunk), i).start()
        return carry

    def start_hold(i, carry):
        hold_move(at(i, chunk), i).start()
        return carry

    @pl.when(odd)
    def _():
        lax.fori_loop(early, passing, start_hold, 0)

    def start_hold_end(amount):
        if amount > int(amount):
            hold_move(span(int(amount), amount), int(amount)).start()

    for_each(after, start_hold_end, odd)

    @pl.when(inner)
    def _():
        raw_below(span(0, early), 0).wait_send()
        tell_row(hello.at[2])
        pl.semaphore_wait(hello.at[2], row_count - 1)
        skip_move(span(ahead, before_first)).start()
        lax.fori_loop(early, chunks, start_first, 0)

    def skip_between(amount):
        skip_move(span(before_first, after_first - given[3] + amount)).start()

    for_each(after, skip_between, inner, (2, 3))

    @pl.when(last)
    def _():
        start_first(chunks - 1, 0)
        skip_move(span(ahead_last, given[1])).start()

    @pl.when(even)
    def _():
        start_first(chunks - 1, 0)

    def give(amount):
        give_move(span(early, amount)).start()

    for_each(after, give, even)

    @pl.when(even)
    def _():
        for i in range(early):
            part = span(i, i + 1)
            raw_below(part, i).wait_recv()
            raw_on(part).start()

    def skip_all(amount):
        skip_move(span(0, amount)).start()

    for_each(second, skip_all, even)

    mix_below(0)
    raw_next(span(0, early)).wait_recv()
    clear()

    def early0(i, carry):
        part = at(i, chunk)
        mixed = transform(1, raw[part, 0:width], raw[part, width:both])
        come0[part] = mixed[:, :width]
        rest[part] = mixed[:, width:]
        add_gram(mixed[:, :width], stay0[part])
        return carry

    lax.fori_loop(0, early, early0, 0)

    def gram1(i, carry):
        part = at(i, chunk)
        first_move(part, i).wait_recv()

        add_gram(come0[part], stay0[part])
        return carry

    lax.fori_loop(early, chunks, gram1, 0)
    def pass_rest(start, stop):
        def pass_on(i, carry):
            part = at(i, chunk)
            hold_move(part, i).wait_recv()
            pass_move(part).start()
            return carry

        @pl.when(even)
        def _():
            lax.fori_loop(early + start, stop, pass_on, 0)

    def pass_end(amount):
        if amount > int(amount):
            part = span(int(amount), amount)
            hold_move(part, int(amount)).wait_recv()
            pass_move(part).start()

    pass_rest(0, early + 1)
    exchange(1)
    pass_rest(1, early + 2)
    for k in range(1, widen):
        if k > 1:
            round_start(k)
        round_end(k)

    def tell(k, carry):
        message(pl.ds(blk, 1), lax.rem(blk + k, blk_count)).start()
        return carry

    lax.fori_loop(1, blk_count, tell, 0)

    def hold_sent(amount):
        hold_move(span(early, amount), early).wait_send()

    def turn1(i, carry):
        part = at(i, chunk)
        mixed = transform(0, come0[part], stay0[part])
        out_ref[part, 0:width] = mixed[:, :width]
        move1[part] = mixed[:, width:]

        @pl.when(jnp.logical_and(i == passing + 1, inner))
        def _():
            for_each(after, hold_sent)

        def skip_end(amount):
            skip_move(span(after_first - given[3] + amount, given[4])).start()

        for_each(after, skip_end, jnp.logical_and(i == passing + 1, inner), (2, 3))

        def begin_second(amount):
            second_move(span(amount, int(amount) + 1)).start()

        for_each(after, begin_second, i == passing + 1)

        @pl.when(i > passing + 1)
        def _():
            second_move(at(i - 1, chunk)).start()

        return carry

    lax.fori_loop(passing, chunks, turn1, 0)
    second_move(span(chunks - 1, chunks)).start()

    pass_rest(2, whole_chunks(second))
    for_each(second, pass_end, even)

    def own1(i, carry):
        part = at(i, chunk)
        out_ref[part, 0:width] = transform(0, come0[part], stay0[part])[:, :width]
        return carry

    lax.fori_loop(0, passing, own1, 0)
    mix_below(1)

    def skip_rest_wait(amount):
        skip_move(span(0, amount)).wait_recv()
        give_move(span(early, amount)).wait_recv()

    for_each(blk, skip_rest_wait)

    def finish_part(part):
        out_ref[part, width:both] = transform(1, skip[part], rest[part])[:, width:]

    def early1(i, carry):
        finish_part(at(i, chunk))
        return carry

    lax.fori_loop(0, own_given, early1, 0)

    def early1_end(amount):
        if amount > int(amount):
            finish_part(span(int(amount), amount))

    for_each(blk, early1_end)
    messages = message(pl.ds(0, blk_count - 1), after)
    messages.wait_recv()
    off_ref[...] = jnp.sum(mgath[...], axis=0) / float(blk_count)

    messages.wait_send()
    first_move(span(early, chunks), early).wait_send()
    for step in range(STEPS):
        cos_move(step).wait_send()

    @pl.when(jnp.logical_not(inner))
    def _():
        raw_next(span(0, early)).wait_send()

    def skip_sent(amount):
        skip_move(span(0, amount)).wait_send()

    for_each(second, skip_sent)

    for_each(after, hold_sent, last)

    @pl.when(even)
    def _():
        raw_on(span(0, early)).wait_send()

    def give_sent(amount):
        give_move(span(early, amount)).wait_send()

    for_each(after, give_sent, even)

    def pass_sent(amount):
        pass_move(span(early, amount)).wait_send()

    for_each(second, pass_sent, even)

    def second_sent(amount):
        second_move(span(amount, chunks)).wait_send()

    for_each(after, second_sent)

    def second_arrived(amount):
        second_move(span(amount, chunks)).wait_recv()

    for_each(blk, second_arrived)


def settle(rotated, off, out_ref, off_ref, scalars, sem):
    whole = pltpu.make_async_copy(rotated, out_ref, sem.at[0])
    whole.start()
    values = off[...]
    lane = lax.broadcasted_iota(jnp.int32, values.shape, 1)
    for step in range(STEPS):
        scalars[step] = jnp.sum(jnp.where(lane == step, values, 0.0))
    few = pltpu.make_async_copy(scalars, off_ref, sem.at[1])
    few.start()
    few.wait()
    whole.wait()


def on_device(row_count, blk_count, matrix):
    rows, both = matrix.shape
    width = both // 2
    chunks, loads, early, given, _, _ = plan = 16, 4, 3, (9, 7.375, 8.625, 9, 7.75), (3, 3.25, 7.25), 2.5
    chunk = rows // chunks
    most = math.ceil(max(given))
    widen = 1
    while 2**widen < blk_count // 2:
        widen += 1
    dma = pltpu.SemaphoreType.DMA
    regular = pltpu.SemaphoreType.REGULAR
    block = pltpu.VMEM((rows, width), F32)
    some = pltpu.VMEM((most * chunk, width), F32)
    few = pltpu.VMEM((early * chunk, both), F32)
    vmem = pl.BlockSpec(memory_space=pltpu.VMEM)
    hbm = pl.BlockSpec(memory_space=pltpu.HBM)
    rotated, off = pl.pallas_call(
        functools.partial(kernel, row_count, blk_count, plan),
        out_shape=(
            jax.ShapeDtypeStruct((rows, both), F32),
            jax.ShapeDtypeStruct((1, width), F32),
        ),
        in_specs=[hbm],
        out_specs=(vmem, vmem),
        scratch_shapes=[
            pltpu.VMEM((rows, both), F32),
            block, block, block, some, block,
            few, few, some, some,
            pltpu.VMEM((both, both), F32),
            pltpu.VMEM((16, width), F32),
            pltpu.VMEM((STEPS, row_count, width + 16, width), F32),
            pltpu.VMEM((2, 2, both, both), BF16),
            pltpu.VMEM((STEPS, width, width), F32),
            pltpu.VMEM((STEPS, width, width), F32),
            pltpu.VMEM((blk_count, 1, width), F32),
            dma((loads,)), dma((early,)), dma((most - early,)), dma((chunks - early,)),
            dma((1,)), dma((2 * STEPS,)), dma((8 + STEPS,)), dma((5 + STEPS,)),
            regular((3,)), regular((widen,)), regular((widen,)),
        ],
        compiler_params=pltpu.CompilerParams(
            collective_id=0, has_side_effects=True, vmem_limit_bytes=48 * 1024 * 1024
        ),
    )(matrix)
    return pl.pallas_call(
        settle,
        out_shape=(
            jax.ShapeDtypeStruct((rows, both), F32),
            jax.ShapeDtypeStruct((STEPS,), F32),
        ),
        in_specs=[vmem, vmem],
        out_specs=(hbm, hbm),
        scratch_shapes=[pltpu.SMEM((STEPS,), F32), dma((2,))],
        compiler_params=pltpu.CompilerParams(vmem_limit_bytes=8 * 1024 * 1024),
    )(rotated, off)


def solution(mesh):
    return jax.shard_map(
        functools.partial(on_device, mesh.shape["row"], mesh.shape["blk"]),
        mesh=mesh,
        in_specs=(P("row", "blk"),),
        out_specs=(P("row", "blk"), P()),
        check_vma=False,
    )
```
